256 devices in a mesh: row: 8 (over z), col: 4 (over x_hi, core), chan: 8 (over x_lo, y).
Axes of the slice: x: 4 (x_hi: 2, x_lo: 2; x = x_hi * 2 + x_lo), y: 4, z: 8, core: 2. Of those that a mesh axis runs over, the one named last changes fastest.
Arguments:
- alignment_features: bfloat16 [2048, 512, 64], P('col', 'row'), may hold values from -8 to 8
- alignment_row_mask: int32 [2048], P('col'), may hold values 0 or 1
- residue_token_mask: int32 [512], P('row'), may hold values 0 or 1
- layer_norm_gain: float32 [64], replicated, may hold values from 0.25 to 1.75
- layer_norm_bias: float32 [64], replicated, may hold values from -3 to 3
- left_factor_weight: bfloat16 [64, 32], P(None, 'chan'), may hold values from -0.75 to 0.75
- right_factor_weight: bfloat16 [64, 32], replicated, may hold values from -0.75 to 0.75
- output_weight: bfloat16 [1024, 128], P('chan'), may hold values from -0.1875 to 0.1875
- output_bias: float32 [128], replicated, may hold values from -3 to 3
Outputs:
- pair_update: bfloat16 [512, 512, 128], P('col', ('row', 'chan'))
The draws below stay inside these ranges and needn't reach their ends.
All inputs are finite; a program needn't handle non-finite values. No bound on the sum of `alignment_row_mask` or of `residue_token_mask` on one device may be relied on, other than what follows from the above.
Results may differ from the reference program's by a relative error of at most 0.0038.
Values may be sent and summed in bfloat16 or wider, within the bound.
No kernel may reach another device: no remote copies, remote signals or barrier semaphores. Data moves between devices by JAX's collectives and lax.ppermute only.
A program may use at most 128 MiB of HBM per device.

```python
import jax
import jax.numpy as jnp
from jax import lax

CM = 64
C_HID = 32
CZ = 128
S = 2048
N = 512


def draw_alignment_features(key, part):
    row_key = jax.random.fold_in(key, 21)
    token_key = jax.random.fold_in(key, 22)
    noise_key = jax.random.fold_in(key, 23)
    strength_key = jax.random.fold_in(key, 24)
    row_factor = jax.random.normal(row_key, (S, CM), jnp.float32)
    token_factor = jax.random.normal(token_key, (N, CM), jnp.float32)
    noise = jax.random.normal(noise_key, (S, N, CM), jnp.float32)
    strength = jnp.exp(jax.random.uniform(strength_key, (S, 1, 1), jnp.float32, -0.7, 1.4))
    values = strength * row_factor[:, None, :] * token_factor[None, :, :] + noise
    return jnp.clip(values, -8.0, 8.0).astype(jnp.bfloat16)


def touch_ends(values, key, smallest, top_value):
    longest = values.shape.index(max(values.shape))
    spots = []
    for shift in (0, 1):
        where = [jax.random.randint(jax.random.fold_in(key, axis), (), 0, length) for axis, length in enumerate(values.shape)]
        where[longest] = (where[longest] + shift) % values.shape[longest]
        spots.append(tuple(where))
    return values.at[spots[0]].set(smallest).at[spots[1]].set(top_value)


def block_levels(own_key, dims, cuts, least, high):
    def one(dim, shards_of):
        heights = jax.random.uniform(jax.random.fold_in(jax.random.fold_in(own_key, 6), dim), (shards_of,), jnp.float32, least / len(cuts), high / len(cuts))
        return jnp.repeat(jnp.exp(heights), dims[dim] // shards_of).reshape((-1,) + (1,) * (len(dims) - dim - 1))

    factor_of = one(*cuts[0])
    for cut in cuts[1:]:
        factor_of = factor_of * one(*cut)
    return factor_of


def bell_draw(stream_key, extent, scale, bound, split=(), held_as=jnp.bfloat16):
    entries = scale * jax.random.normal(stream_key, extent, jnp.float32)
    if split:
        entries = entries * block_levels(stream_key, extent, split, -0.22, 0.18)
    return jnp.clip(entries, -bound, bound).astype(held_as)


def setup_inputs(seed: int = 0) -> dict:
    splits = jax.random.split(jax.random.key(seed), 10)
    alignment_features = draw_alignment_features(jax.random.fold_in(splits[9], 71), 0)
    alignment_row_mask = touch_ends((jax.random.randint(splits[1], (S,), 0, 8) < 7).astype(jnp.int32), jax.random.fold_in(splits[1], 1), 0, 1)
    residue_token_mask = touch_ends((jax.random.randint(splits[2], (N,), 0, 8) < 7).astype(jnp.int32), jax.random.fold_in(splits[2], 1), 0, 1)
    layer_norm_gain = jnp.clip(1.0 + 0.15 * jax.random.normal(splits[3], (CM,), jnp.float32), 0.25, 1.75)
    layer_norm_bias = bell_draw(splits[4], (CM,), 0.5, 3.0, (), jnp.float32)
    left_factor_weight = bell_draw(splits[5], (CM, C_HID), CM ** -0.5, 0.75, ((1, 8),))
    right_factor_weight = bell_draw(splits[6], (CM, C_HID), CM ** -0.5, 0.75)
    output_weight = bell_draw(splits[7], (C_HID * C_HID, CZ), (C_HID * C_HID) ** -0.5, 0.1875, ((0, 8),))
    output_bias = bell_draw(splits[8], (CZ,), 0.5, 3.0, (), jnp.float32)
    return {"alignment_features": alignment_features, "alignment_row_mask": alignment_row_mask, "residue_token_mask": residue_token_mask, "layer_norm_gain": layer_norm_gain, "layer_norm_bias": layer_norm_bias, "left_factor_weight": left_factor_weight, "right_factor_weight": right_factor_weight, "output_weight": output_weight, "output_bias": output_bias}


def apply_layer_norm(features, layer_norm_gain, layer_norm_bias):
    values = features.astype(jnp.float32)
    center = values - lax.optimization_barrier(jnp.mean(values, axis=-1, keepdims=True))
    spread = lax.optimization_barrier(jnp.mean(center * center, axis=-1, keepdims=True))
    return (center * lax.rsqrt(spread + 1e-05) * layer_norm_gain + layer_norm_bias).astype(jnp.bfloat16)

def reference(alignment_features, alignment_row_mask, residue_token_mask, layer_norm_gain, layer_norm_bias, left_factor_weight, right_factor_weight, output_weight, output_bias):
    normalized_features = apply_layer_norm(alignment_features, layer_norm_gain, layer_norm_bias).astype(jnp.float32)
    weight = alignment_row_mask[:, None].astype(jnp.float32) * residue_token_mask[None, :].astype(jnp.float32)
    left = (jnp.einsum('stm,mc->stc', normalized_features, left_factor_weight.astype(jnp.float32)) * weight[:, :, None]).astype(jnp.bfloat16)
    right = (jnp.einsum('stm,me->ste', normalized_features, right_factor_weight.astype(jnp.float32)) * weight[:, :, None]).astype(jnp.bfloat16)
    row_total = jnp.sum(alignment_row_mask).astype(jnp.float32)
    token_float = residue_token_mask.astype(jnp.float32)
    count = jnp.maximum(row_total * token_float[:, None] * token_float[None, :], 1.0)
    step_size = min(64, N)
    left_blocks = left.reshape(S, N // step_size, step_size, C_HID).transpose(1, 0, 2, 3)
    right_float = right.astype(jnp.float32)

    def one_block(left_block):
        outer = jnp.einsum('sic,sje->ijce', left_block.astype(jnp.float32), right_float).astype(jnp.bfloat16)
        flat_outer = outer.reshape(step_size * N, C_HID * C_HID)
        return jnp.dot(flat_outer, output_weight, preferred_element_type=jnp.float32).reshape(step_size, N, CZ)
    projected = lax.map(one_block, left_blocks).reshape(N, N, CZ)
    return ((projected + output_bias) / count[:, :, None]).astype(jnp.bfloat16)
```

```python
import functools

import jax
import jax.numpy as jnp
from jax import lax
from jax.experimental import pallas as pl
from jax.experimental.pallas import tpu as pltpu
from jax.sharding import PartitionSpec as P

F32 = jnp.float32
BF16 = jnp.bfloat16
VMEM = pl.BlockSpec(memory_space=pltpu.VMEM)
ANY = pl.BlockSpec(memory_space=pl.ANY)

S = 512
N = 64
M = 64
C = 32
Z = 128
T = 8
ROWS = N * T
EXTRA = 8


def column_of(row):
    n = row.shape[1]
    r = lax.broadcasted_iota(jnp.int32, (n, n), 0)
    c = lax.broadcasted_iota(jnp.int32, (n, n), 1)
    return jnp.sum(jnp.where(r == c, jnp.broadcast_to(row, (n, n)), 0.0), axis=1, keepdims=True)


def normalize(x, gain, bias):
    values = x.astype(F32)
    center = values - jnp.mean(values, axis=1, keepdims=True)
    spread = jnp.mean(center * center, axis=1, keepdims=True)
    return center * lax.rsqrt(spread + 1e-05) * gain[None] + bias[None]


def right_kernel(x_ref, row_ref, tok_ref, gain_ref, bias_ref, wr_ref, wl_ref, wo_ref, out_ref, pack_ref, buf, sem):
    k = lax.axis_index("chan")
    copy = pltpu.make_async_copy(x_ref.at[pl.ds(k * T, T)], buf, sem)
    copy.start()
    pack_ref[0:Z, :] = wo_ref[...]
    pack_ref[Z : Z + 16, :] = jnp.zeros((16, Z), BF16)
    pack_ref[Z : Z + 4, 0:M] = wl_ref[...]
    gain = column_of(gain_ref[...])
    bias = column_of(bias_ref[...])
    token = tok_ref[...].astype(F32)
    t_iota = lax.broadcasted_iota(jnp.int32, (T, N), 0)
    l_iota = lax.broadcasted_iota(jnp.int32, (T, N), 1)
    token_col = jnp.sum(
        jnp.where(l_iota == t_iota + k * T, jnp.broadcast_to(token, (T, N)), 0.0), axis=1, keepdims=True
    )
    weight = token_col * row_ref[...].astype(F32)
    copy.wait()
    normed = normalize(buf[...], gain, bias).astype(BF16)
    wr = wr_ref[...]
    for t in range(T):
        part = jnp.dot(wr, normed[t], preferred_element_type=F32)
        out_ref[t * C : (t + 1) * C, :] = (part * weight[t : t + 1]).astype(BF16)
    pad = jnp.concatenate([jnp.broadcast_to(token_col, (T, S)), jnp.zeros((T, S), F32)], axis=0)
    out_ref[T * C :, :] = pad.astype(BF16)


def norm_kernel(x_ref, row_ref, tok_ref, gain_ref, bias_ref, out_ref):
    step = pl.program_id(0)
    gain = column_of(gain_ref[...])
    bias = column_of(bias_ref[...])
    token = tok_ref[...].astype(F32)
    t_iota = lax.broadcasted_iota(jnp.int32, (T, N), 0)
    l_iota = lax.broadcasted_iota(jnp.int32, (T, N), 1)
    token_col = jnp.sum(
        jnp.where(l_iota == t_iota + step * T, jnp.broadcast_to(token, (T, N)), 0.0), axis=1, keepdims=True
    )
    weight = token_col * row_ref[...].astype(F32)
    normed = normalize(x_ref[...], gain, bias)
    out_ref[...] = (normed * weight[:, None, :]).astype(BF16).reshape(T * M, S)


def left_kernel(n_ref, wl_ref, out_ref, wide):
    @pl.when(pl.program_id(0) == 0)
    def _():
        rep = (
            lax.broadcasted_iota(jnp.int32, (C * T, C), 0) // T
            == lax.broadcasted_iota(jnp.int32, (C * T, C), 1)
        ).astype(F32).astype(BF16)
        tile = (
            lax.broadcasted_iota(jnp.int32, (M, T * M), 0)
            == lax.broadcasted_iota(jnp.int32, (M, T * M), 1) % M
        ).astype(F32).astype(BF16)
        tall = jnp.dot(rep, wl_ref[...], preferred_element_type=F32).astype(BF16)
        full = jnp.dot(tall, tile, preferred_element_type=F32)
        own = (
            lax.broadcasted_iota(jnp.int32, (C * T, T * M), 0) % T
            == lax.broadcasted_iota(jnp.int32, (C * T, T * M), 1) // M
        )
        wide[...] = jnp.where(own, full, 0.0).astype(BF16)

    part = jnp.dot(wide[...], n_ref[...], preferred_element_type=F32)
    out_ref[...] = part.reshape(C, T, S).astype(BF16)


def pair_block(load, token_rows, lf_ref, w2_ref, row_ref, spread, store):
    for n in range(8):
        for h in range(2):
            part = lax.dot_general(
                load(h),
                lf_ref[n * 256 : (n + 1) * 256, :],
                (((1,), (1,)), ((), ())),
                preferred_element_type=F32,
            ).astype(BF16)
            for q in range(4):
                t = h * 4 + q
                for u in range(2):
                    hi = n * 2 + u
                    spread[t // 2, hi * C : (hi + 1) * C, (t % 2) * 128 : (t % 2) * 128 + 128] = part[
                        q * C : (q + 1) * C, u * 128 : (u + 1) * 128
                    ]
    low = lax.broadcasted_iota(jnp.int32, (Z, 128), 1) < N
    for p in range(T // 2):
        both = jnp.dot(w2_ref[...], spread[p], preferred_element_type=F32)
        x0, y0 = both[:Z, :128], both[Z:, :128]
        x1, y1 = both[:Z, 128:], both[Z:, 128:]
        pair = jnp.where(low, x0, y1) + pltpu.roll(jnp.where(low, x1, y0), N, 1)
        flat = pair.T
        store(pl.ds(2 * p, N, stride=T), flat[:N])
        store(pl.ds(2 * p + 1, N, stride=T), flat[N:])
    rows_used = jnp.sum(row_ref[...].astype(F32), axis=1, keepdims=True)
    lane = lax.broadcasted_iota(jnp.int32, (EXTRA, Z), 1)
    mask = jnp.broadcast_to(token_rows().astype(F32)[:EXTRA, :1], (EXTRA, Z))
    store(pl.ds(ROWS, EXTRA), jnp.where(lane < N, jnp.broadcast_to(rows_used, (EXTRA, Z)), mask))


def whole(ref):
    return (lambda h: ref[h * 128 : (h + 1) * 128, :]), (lambda: ref[T * C :, :])


def halves(first, second):
    return (lambda h: first[...] if h == 0 else second[0:128, :]), (lambda: second[128:, :])


def first_kernel(own, lf, w2, row, out, spread):
    def store(where, value):
        out[where, :] = value

    pair_block(*whole(own), lf, w2, row, spread, store)


def core_kept(offset):
    block = lax.rem(lax.axis_index("row") + offset + 8, 8)
    return lax.rem(block // 2, 2) == lax.rem(lax.axis_index("col"), 2)


def x_kept(offset):
    block = lax.rem(lax.axis_index("row") + offset + 8, 8)
    return block // 4 == lax.axis_index("col") // 2


def keep_or_send(kept, make, send, keep):
    @pl.when(kept)
    def _():
        make(keep)

    @pl.when(jnp.logical_not(kept))
    def _():
        make(send)


def two_kernel(offset, back, ahead, lf, w2, row, out, spread):
    kept = core_kept(offset).astype(jnp.int32)

    def store_ahead(where, value):
        out[kept, where, :] = value

    def store_back(where, value):
        out[1 - kept, where, :] = value

    pair_block(*whole(back), lf, w2, row, spread, store_back)
    pair_block(*whole(ahead), lf, w2, row, spread, store_ahead)


def mixed_kernel(back, ahead, base, lf, w2, row, out, rest, spread):
    kept = core_kept(2).astype(jnp.int32)

    def store_ahead(where, value):
        out[kept, where, :] = value

    def store_back(where, value):
        rest[where, :] = value

    out[1 - kept, :, :] = base[...]
    pair_block(*whole(ahead), lf, w2, row, spread, store_ahead)
    pair_block(*whole(back), lf, w2, row, spread, store_back)


def last_kernel(first, second, rest, lf, w2, row, out, spread):
    kept = core_kept(4).astype(jnp.int32)

    def store(where, value):
        out[kept, where, :] = value

    out[1 - kept, :, :] = rest[...]
    pair_block(*halves(first, second), lf, w2, row, spread, store)


def add_kernel(a_offsets, keep_a, got_a, keep_b, got_b, out):
    first, second = a_offsets
    kept = jnp.where(core_kept(first), x_kept(first), x_kept(second)).astype(jnp.int32)
    out[kept, :, :] = keep_a[...] + got_a[...]
    out[1 - kept, :, :] = keep_b[...] + got_b[...]


def final_kernel(keep, got, tok_ref, bias_ref, out):
    total = keep[...] + got[...]
    tail = total[ROWS:, :]
    rows_used = tail[0:1, 0:1]
    second = (tail[:, N : N + 1] > 0.0).astype(F32)
    first = column_of(tok_ref[...].astype(F32))
    count = jnp.maximum(rows_used[None] * first[:, :, None] * second[None], 1.0)
    pairs = total[:ROWS, :].reshape(N, T, Z)
    out[...] = ((pairs + bias_ref[...][None]) / count).astype(BF16)


def call(kernel, out, *args, specs=None, scratch=(), flops=0, **kw):
    leaves = jax.tree.leaves(out)
    bytes_accessed = sum(a.size * a.dtype.itemsize for a in list(args) + leaves)
    return pl.pallas_call(
        kernel,
        out_shape=out,
        in_specs=specs or [VMEM] * len(args),
        out_specs=jax.tree.map(lambda _: VMEM, out),
        scratch_shapes=scratch,
        cost_estimate=pl.CostEstimate(flops=flops, bytes_accessed=bytes_accessed, transcendentals=0),
        **kw,
    )(*args)


def shape(dims, dtype):
    return jax.ShapeDtypeStruct(dims, dtype)


def body(x, row_mask, token_mask, gain, bias, wl, wr, wo, out_bias):
    xt = x.transpose(1, 2, 0)
    row = row_mask.reshape(1, S)
    tok = token_mask.reshape(1, N)
    gain, bias = gain.reshape(1, M), bias.reshape(1, M)

    ring = [[(i, (i + d) % 8) for i in range(8)] for d in (1, -1)]
    y_ring = [[(a * 4 + b, a * 4 + (b + d) % 4) for a in range(2) for b in range(4)] for d in (1, -1)]
    x_swap = [(c, (c + 4) % 8) for c in range(8)]
    core_swap = [(0, 1), (1, 0), (2, 3), (3, 2)]
    xh_swap = [(0, 2), (1, 3), (2, 0), (3, 1)]

    own, pack = call(
        right_kernel,
        (shape((T * C + 16, S), BF16), shape((Z + 16, Z), BF16)),
        xt, row, tok, gain, bias, wr.T, wl.T, wo,
        specs=[ANY] + [VMEM] * 7,
        scratch=[pltpu.VMEM((T, M, S), BF16), pltpu.SemaphoreType.DMA(())],
    )

    ahead, back = own, own
    from_back, from_ahead = [], []
    for _ in range(3):
        back = lax.ppermute(back, "row", ring[0])
        ahead = lax.ppermute(ahead, "row", ring[1])
        from_back.append(back)
        from_ahead.append(ahead)
    half_a = lax.ppermute(back[:128], "row", ring[0])
    half_b = lax.ppermute(ahead[128:], "row", ring[1])

    up = lax.ppermute(pack, "chan", y_ring[0])
    down = lax.ppermute(pack, "chan", y_ring[1])
    over = lax.ppermute(up, "chan", y_ring[0])
    four = jnp.stack([pack, up, down, over])
    other = lax.ppermute(four, "chan", x_swap)
    packs = jnp.concatenate([four, other], axis=0)
    wl_all = packs[:, Z : Z + 4, :M].reshape(8, 2, 2, M).transpose(0, 2, 1, 3).reshape(C, M)
    w2 = packs[:, :Z, :].reshape(8, 2, 64, Z).transpose(1, 3, 0, 2).reshape(2 * Z, 512)

    normed = pl.pallas_call(
        norm_kernel,
        grid=(N // T,),
        out_shape=shape((N * M, S), BF16),
        in_specs=[
            pl.BlockSpec((T, M, S), lambda i: (i, 0, 0)),
            pl.BlockSpec((1, S), lambda i: (0, 0)),
            pl.BlockSpec((1, N), lambda i: (0, 0)),
            pl.BlockSpec((1, M), lambda i: (0, 0)),
            pl.BlockSpec((1, M), lambda i: (0, 0)),
        ],
        out_specs=pl.BlockSpec((T * M, S), lambda i: (i, 0)),
        cost_estimate=pl.CostEstimate(flops=30_000_000, bytes_accessed=8 << 20, transcendentals=0),
    )(xt, row, tok, gain, bias)
    left = pl.pallas_call(
        left_kernel,
        grid=(N // T,),
        out_shape=shape((C, N, S), BF16),
        in_specs=[
            pl.BlockSpec((T * M, S), lambda i: (i, 0)),
            pl.BlockSpec((C, M), lambda i: (0, 0)),
        ],
        out_specs=pl.BlockSpec((C, T, S), lambda i: (0, i, 0)),
        scratch_shapes=[pltpu.VMEM((C * T, T * M), BF16)],
        cost_estimate=pl.CostEstimate(flops=1 << 30, bytes_accessed=6 << 20, transcendentals=0),
    )(normed, wl_all)
    lf = left.reshape(C * N, S)

    block = shape((ROWS + EXTRA, Z), F32)
    pair = shape((2, ROWS + EXTRA, Z), F32)
    spread = [pltpu.VMEM((T // 2, 512, 256), BF16)]
    one = 800 << 20
    p0 = call(first_kernel, block, own, lf, w2, row, scratch=spread, flops=one)
    p1 = call(functools.partial(two_kernel, 1), pair, from_back[0], from_ahead[0], lf, w2, row, scratch=spread, flops=2 * one)
    p2, rest = call(mixed_kernel, (pair, block), from_back[1], from_ahead[1], p0, lf, w2, row, scratch=spread, flops=2 * one)
    p3 = call(functools.partial(two_kernel, 3), pair, from_back[2], from_ahead[2], lf, w2, row, scratch=spread, flops=2 * one)
    p4 = call(last_kernel, pair, half_a, half_b, rest, lf, w2, row, scratch=spread, flops=one)

    e1 = lax.ppermute(p1[0], "col", core_swap)
    e2 = lax.ppermute(p2[0], "col", core_swap)
    e3 = lax.ppermute(p3[0], "col", core_swap)
    e4 = lax.ppermute(p4[0], "col", core_swap)
    odd = call(functools.partial(add_kernel, (1, -1)), pair, p1[1], e1, p3[1], e3)
    even = call(functools.partial(add_kernel, (0, 2)), pair, p2[1], e2, p4[1], e4)
    f1 = lax.ppermute(odd[0], "col", xh_swap)
    f2 = lax.ppermute(even[0], "col", xh_swap)
    part = shape((N, T, Z), BF16)
    out_bias = out_bias.reshape(1, Z)
    y1 = call(final_kernel, part, odd[1], f1, tok, out_bias)
    y2 = call(final_kernel, part, even[1], f2, tok, out_bias)

    def home(p):
        return [
            (z * 4 + c, (2 * c + ((z % 2) ^ p)) * 4 + z // 2) for z in range(8) for c in range(4)
        ]

    g1 = lax.ppermute(y1, ("row", "col"), home(1))
    g2 = lax.ppermute(y2, ("row", "col"), home(0))
    low_row = lax.axis_index("row") % 2 == 0
    return jnp.where(low_row, jnp.concatenate([g2, g1], 0), jnp.concatenate([g1, g2], 0))


def solution(mesh):
    in_specs = (
        P("col", "row", None),
        P("col"),
        P("row"),
        P(),
        P(),
        P(None, "chan"),
        P(),
        P("chan", None),
        P(),
    )
    out_specs = P("col", ("row", "chan"), None)
    return jax.shard_map(body, mesh=mesh, in_specs=in_specs, out_specs=out_specs, check_vma=False)
```

```python
import functools

import jax
import jax.numpy as jnp
from jax import lax
from jax.experimental import pallas as pl
from jax.experimental.pallas import tpu as pltpu
from jax.sharding import PartitionSpec as P


F32 = jnp.float32
BF16 = jnp.bfloat16
VMEM = pl.BlockSpec(memory_space=pltpu.VMEM)
HBM = pl.BlockSpec(memory_space=pltpu.HBM)

S = 512
N = 64
M = 64
C = 32
Z = 128
T = 8
ROWS = N * T
EXTRA = 8


def column_of(row):
    n = row.shape[1]
    r = lax.broadcasted_iota(jnp.int32, (n, n), 0)
    c = lax.broadcasted_iota(jnp.int32, (n, n), 1)
    return jnp.sum(jnp.where(r == c, jnp.broadcast_to(row, (n, n)), 0.0), axis=1, keepdims=True)


def normalize(x, gain, bias):
    values = x.astype(F32)
    center = values - jnp.mean(values, axis=1, keepdims=True)
    spread = jnp.mean(center * center, axis=1, keepdims=True)
    return center * lax.rsqrt(spread + 1e-05) * gain[None] + bias[None]


def tokens_of(tok_ref, start, count):
    token = tok_ref[...].astype(F32)
    t_iota = lax.broadcasted_iota(jnp.int32, (count, N), 0)
    l_iota = lax.broadcasted_iota(jnp.int32, (count, N), 1)
    return jnp.sum(
        jnp.where(l_iota == t_iota + start, jnp.broadcast_to(token, (count, N)), 0.0), axis=1, keepdims=True
    )


def pack_kernel(wl_ref, wo_ref, out_ref):
    out_ref[0:Z, :] = wo_ref[...]
    out_ref[Z : Z + 16, :] = jnp.zeros((16, Z), BF16)
    out_ref[Z : Z + 4, 0:M] = wl_ref[...]


def stack_kernel(a, b, c, d, out):
    for i, ref in enumerate((a, b, c, d)):
        out[i] = ref[...]


def weight_kernel(near, far, wl_out, w2_out):
    packs = [near[i] for i in range(4)] + [far[i] for i in range(4)]
    for i in range(0, 8, 2):
        a, b = (packs[i + j][:Z, :].astype(F32).T.astype(BF16) for j in range(2))
        w2_out[:Z, i * 64 : i * 64 + 128] = jnp.concatenate([a[:, :64], b[:, :64]], axis=1)
        w2_out[Z:, i * 64 : i * 64 + 128] = jnp.concatenate([a[:, 64:], b[:, 64:]], axis=1)
    lefts = jnp.concatenate([pack[Z:, :M] for pack in packs], axis=0)
    r = lax.broadcasted_iota(jnp.int32, (C, 128), 0)
    c = lax.broadcasted_iota(jnp.int32, (C, 128), 1)
    pick = c == r // 4 * 16 + r % 2 * 2 + r // 2 % 2
    wl_out[...] = jnp.dot(pick.astype(F32).astype(BF16), lefts, preferred_element_type=F32).astype(BF16)


def right_kernel(x_ref, row_ref, tok_ref, gain_ref, bias_ref, wr_ref, out_ref, buf, sem):
    k = lax.axis_index("chan")
    copy = pltpu.make_async_copy(x_ref.at[pl.ds(k * T, T)], buf, sem)
    copy.start()
    gain = column_of(gain_ref[...])
    bias = column_of(bias_ref[...])
    token_col = tokens_of(tok_ref, k * T, T)
    weight = token_col * row_ref[...].astype(F32)
    wr = wr_ref[...]
    pad = jnp.concatenate([jnp.broadcast_to(token_col, (T, S)), jnp.zeros((T, S), F32)], axis=0)
    out_ref[T * C :, :] = pad.astype(BF16)
    copy.wait()
    for t in range(T):
        normed = normalize(buf[t : t + 1], gain, bias).astype(BF16)
        part = jnp.dot(wr, normed[0], preferred_element_type=F32)
        out_ref[t * C : (t + 1) * C, :] = (part * weight[t : t + 1]).astype(BF16)


def norm_kernel(half, x_ref, gain_ref, bias_ref, out_ref, buf, sems):
    copies = [
        pltpu.make_async_copy(x_ref.at[pl.ds(half * N // 2 + g * T, T)], buf.at[g], sems.at[g])
        for g in range(N // 2 // T)
    ]
    for copy in copies:
        copy.start()
    gain = column_of(gain_ref[...])
    bias = column_of(bias_ref[...])
    for g, copy in enumerate(copies):
        copy.wait()

        def one(t, carry):
            normed = normalize(buf[g, pl.ds(t, 1)], gain, bias)
            out_ref[pl.ds(pl.multiple_of((g * T + t) * M, M), M), :] = normed[0].astype(BF16)
            return carry

        lax.fori_loop(0, T, one, 0)


def left_kernel(n_a, n_b, wl_ref, row_ref, tok_ref, out_ref):
    rep = (
        lax.broadcasted_iota(jnp.int32, (C * T, C), 0) // T == lax.broadcasted_iota(jnp.int32, (C * T, C), 1)
    ).astype(F32).astype(BF16)
    tile = (
        lax.broadcasted_iota(jnp.int32, (M, T * M), 0) == lax.broadcasted_iota(jnp.int32, (M, T * M), 1) % M
    ).astype(F32).astype(BF16)
    tall = jnp.dot(rep, wl_ref[...], preferred_element_type=F32).astype(BF16)
    full = jnp.dot(tall, tile, preferred_element_type=F32)
    own = (
        lax.broadcasted_iota(jnp.int32, (C * T, T * M), 0) % T
        == lax.broadcasted_iota(jnp.int32, (C * T, T * M), 1) // M
    )
    wide = jnp.where(own, full, 0.0).astype(BF16)
    rows = row_ref[...].astype(F32)
    for g in range(N // T):
        weight = tokens_of(tok_ref, g * T, T) * rows
        n_ref, at = (n_a, g) if g < N // T // 2 else (n_b, g - N // T // 2)
        part = jnp.dot(wide, n_ref[at * T * M : (at + 1) * T * M, :], preferred_element_type=F32)
        out_ref[:, g * T : (g + 1) * T, :] = (part.reshape(C, T, S) * weight[None]).astype(BF16)


def pair_blocks(blocks, lf_ref, w2_ref, row_ref, spread):
    rhs = jnp.concatenate([rows for rows, _, _ in blocks], axis=0) if len(blocks) > 1 else blocks[0][0]
    for n in range(8):
        part = lax.dot_general(
            rhs, lf_ref[n * 256 : (n + 1) * 256, :], (((1,), (1,)), ((), ())), preferred_element_type=F32
        ).astype(BF16)
        for b in range(len(blocks)):
            for t in range(T):
                for u in range(2):
                    hi = n * 2 + u
                    spread[b * T // 2 + t // 2, hi * C : (hi + 1) * C, (t % 2) * 128 : (t % 2) * 128 + 128] = part[
                        (b * T + t) * C : (b * T + t + 1) * C, u * 128 : (u + 1) * 128
                    ]
    low = lax.broadcasted_iota(jnp.int32, (Z, 128), 1) < N
    rows_used = jnp.sum(row_ref[...].astype(F32), axis=1, keepdims=True)
    lane = lax.broadcasted_iota(jnp.int32, (EXTRA, Z), 1)
    w2 = w2_ref[...]
    for b, (_, extra, store) in enumerate(blocks):
        for p in range(T // 2):
            both = jnp.dot(w2, spread[b * T // 2 + p], preferred_element_type=F32)
            x0, y0 = both[:Z, :128], both[Z:, :128]
            x1, y1 = both[:Z, 128:], both[Z:, 128:]
            pair = jnp.where(low, x0, y1) + pltpu.roll(jnp.where(low, x1, y0), N, 1)
            flat = pair.T
            store(pl.ds(2 * p, N, stride=T), flat[:N])
            store(pl.ds(2 * p + 1, N, stride=T), flat[N:])
        mask = jnp.broadcast_to(extra.astype(F32)[:EXTRA, :1], (EXTRA, Z))
        store(pl.ds(ROWS, EXTRA), jnp.where(lane < N, jnp.broadcast_to(rows_used, (EXTRA, Z)), mask))


def whole(ref):
    return ref[: T * C, :], ref[T * C :, :]


def halves(first, second):
    return jnp.concatenate([first[...], second[:128, :]], axis=0), second[128:, :]


def to(ref):
    def store(where, value):
        ref[where, :] = value

    return store


def to_either(kept, keep, send):
    def store(where, value):
        @pl.when(kept)
        def _():
            keep[where, :] = value

        @pl.when(jnp.logical_not(kept))
        def _():
            send[where, :] = value

    return store


def not_kept(kept):
    return jnp.logical_not(kept)


def core_kept(offset):
    block = lax.rem(lax.axis_index("row") + offset + 8, 8)
    return lax.rem(block // 2, 2) == lax.rem(lax.axis_index("col"), 2)


def x_kept(offset):
    block = lax.rem(lax.axis_index("row") + offset + 8, 8)
    return block // 4 == lax.axis_index("col") // 2


def first_kernel(own, lf, w2, row, out, spread):
    pair_blocks([whole(own) + (to(out),)], lf, w2, row, spread)


def two_kernel(offset, back, ahead, lf, w2, row, keep, send, spread):
    kept = core_kept(offset)
    pair_blocks(
        [
            whole(back) + (to_either(not_kept(kept), keep, send),),
            whole(ahead) + (to_either(kept, keep, send),),
        ],
        lf, w2, row, spread,
    )


def copy_either(kept, value, keep, send):
    @pl.when(kept)
    def _():
        keep[...] = value[...]

    @pl.when(jnp.logical_not(kept))
    def _():
        send[...] = value[...]


def mixed_kernel(back, ahead, base, lf, w2, row, keep, send, rest, spread):
    kept = core_kept(2)
    copy_either(not_kept(kept), base, keep, send)
    pair_blocks(
        [whole(back) + (to(rest),), whole(ahead) + (to_either(kept, keep, send),)], lf, w2, row, spread
    )


def last_kernel(first, second, rest, lf, w2, row, keep, send, spread):
    kept = core_kept(4)
    copy_either(not_kept(kept), rest, keep, send)
    pair_blocks([halves(first, second) + (to_either(kept, keep, send),)], lf, w2, row, spread)


def add_kernel(a_offsets, keep_a, got_a, keep_b, got_b, keep, send):
    first, second = a_offsets
    kept = jnp.where(core_kept(first), x_kept(first), x_kept(second))

    @pl.when(kept)
    def _():
        keep[...] = keep_a[...] + got_a[...]
        send[...] = keep_b[...] + got_b[...]

    @pl.when(jnp.logical_not(kept))
    def _():
        send[...] = keep_a[...] + got_a[...]
        keep[...] = keep_b[...] + got_b[...]


def final_kernel(keep, got, tok_ref, bias_ref, out):
    total = keep[...] + got[...]
    tail = total[ROWS:, :]
    rows_used = tail[0:1, 0:1]
    second = (tail[:, N : N + 1] > 0.0).astype(F32)
    first = column_of(tok_ref[...].astype(F32))
    count = jnp.maximum(rows_used[None] * first[:, :, None] * second[None], 1.0)
    pairs = total[:ROWS, :].reshape(N, T, Z)
    out[...] = ((pairs + bias_ref[...][None]) / count).astype(BF16)


def call(kernel, out, *args, specs=None, scratch=(), flops=0, limit=10):
    leaves = jax.tree.leaves(out)
    bytes_accessed = sum(a.size * a.dtype.itemsize for a in list(args) + leaves)
    return pl.pallas_call(
        kernel,
        out_shape=out,
        in_specs=specs or [VMEM] * len(args),
        out_specs=jax.tree.map(lambda _: VMEM, out),
        scratch_shapes=scratch,
        compiler_params=pltpu.CompilerParams(vmem_limit_bytes=limit << 20),
        cost_estimate=pl.CostEstimate(flops=flops, bytes_accessed=bytes_accessed, transcendentals=0),
    )(*args)


def shape(dims, dtype):
    return jax.ShapeDtypeStruct(dims, dtype)


def program(x, row_mask, token_mask, gain, bias, wl, wr, wo, out_bias):
    xt = pltpu.with_memory_space_constraint(x.transpose(1, 2, 0), pltpu.HBM)
    row = row_mask.reshape(1, S)
    tok = token_mask.reshape(1, N)
    gain, bias = gain.reshape(1, M), bias.reshape(1, M)

    ring = [[(i, (i + d) % 8) for i in range(8)] for d in (1, -1)]
    y_ring = {d: [(a * 4 + b, a * 4 + (b + d) % 4) for a in range(2) for b in range(4)] for d in (1, -1, 2)}
    x_swap = [(c, (c + 4) % 8) for c in range(8)]
    core_swap = [(0, 1), (1, 0), (2, 3), (3, 2)]
    xh_swap = [(0, 2), (1, 3), (2, 0), (3, 1)]

    pack = call(pack_kernel, shape((Z + 16, Z), BF16), wl.T, wo)
    up = lax.ppermute(pack, "chan", y_ring[1])
    down = lax.ppermute(pack, "chan", y_ring[-1])
    over = lax.ppermute(pack, "chan", y_ring[2])
    four = call(stack_kernel, shape((4, Z + 16, Z), BF16), pack, up, down, over, limit=4)
    other = lax.ppermute(four, "chan", x_swap)
    wl_all, w2 = call(weight_kernel, (shape((C, M), BF16), shape((2 * Z, 512), BF16)), four, other, limit=4)

    own = call(
        right_kernel, shape((T * C + 16, S), BF16), xt, row, tok, gain, bias, wr.T,
        specs=[HBM] + [VMEM] * 5,
        scratch=[pltpu.VMEM((T, M, S), BF16), pltpu.SemaphoreType.DMA(())],
        flops=20 << 20, limit=8,
    )

    ahead, back = own, own
    from_back, from_ahead = [], []
    for _ in range(3):
        back = lax.ppermute(back, "row", ring[0])
        ahead = lax.ppermute(ahead, "row", ring[1])
        from_back.append(back)
        from_ahead.append(ahead)
    half_a = lax.ppermute(back[:128], "row", ring[0])
    half_b = lax.ppermute(ahead[128:], "row", ring[1])

    normed = [
        call(
            functools.partial(norm_kernel, half), shape((N * M // 2, S), BF16), xt, gain, bias,
            specs=[HBM, VMEM, VMEM],
            scratch=[pltpu.VMEM((N // 2 // T, T, M, S), BF16), pltpu.SemaphoreType.DMA((N // 2 // T,))],
            flops=15 << 20, limit=8,
        )
        for half in range(2)
    ]
    left = call(left_kernel, shape((C, N, S), BF16), *normed, wl_all, row, tok, flops=1 << 30, limit=8)
    lf = left.reshape(C * N, S)

    block = shape((ROWS + EXTRA, Z), F32)
    pair = (block, block)
    one = 800 << 20
    shared = (lf, w2, row)

    def spread(n):
        return [pltpu.VMEM((n * T // 2, 512, 256), BF16)]

    p0 = call(first_kernel, block, own, *shared, scratch=spread(1), flops=one)
    k1, s1 = call(functools.partial(two_kernel, 1), pair, from_back[0], from_ahead[0], *shared, scratch=spread(2), flops=2 * one)
    k2, s2, rest = call(mixed_kernel, (block,) * 3, from_back[1], from_ahead[1], p0, *shared, scratch=spread(2), flops=2 * one)
    k3, s3 = call(functools.partial(two_kernel, 3), pair, from_back[2], from_ahead[2], *shared, scratch=spread(2), flops=2 * one)
    k4, s4 = call(last_kernel, pair, half_a, half_b, rest, *shared, scratch=spread(1), flops=one)

    e1 = lax.ppermute(s1, "col", core_swap)
    e2 = lax.ppermute(s2, "col", core_swap)
    e3 = lax.ppermute(s3, "col", core_swap)
    e4 = lax.ppermute(s4, "col", core_swap)
    odd, odd_sent = call(functools.partial(add_kernel, (1, -1)), pair, k1, e1, k3, e3)
    f1 = lax.ppermute(odd_sent, "col", xh_swap)
    even, even_sent = call(functools.partial(add_kernel, (0, 2)), pair, k2, e2, k4, e4)
    f2 = lax.ppermute(even_sent, "col", xh_swap)
    part = shape((N, T, Z), BF16)
    out_bias = out_bias.reshape(1, Z)
    y1 = call(final_kernel, part, odd, f1, tok, out_bias)
    y2 = call(final_kernel, part, even, f2, tok, out_bias)

    def home(p):
        return [(z * 4 + c, (2 * c + ((z % 2) ^ p)) * 4 + z // 2) for z in range(8) for c in range(4)]

    g1 = lax.ppermute(y1, ("row", "col"), home(1))
    g2 = lax.ppermute(y2, ("row", "col"), home(0))
    low_row = lax.axis_index("row") % 2 == 0
    return jnp.where(low_row, jnp.concatenate([g2, g1], 0), jnp.concatenate([g1, g2], 0))


def solution(mesh):
    in_specs = (
        P("col", "row", None),
        P("col"),
        P("row"),
        P(),
        P(),
        P(None, "chan"),
        P(),
        P("chan", None),
        P(),
    )
    out_specs = P("col", ("row", "chan"), None)
    return jax.shard_map(program, mesh=mesh, in_specs=in_specs, out_specs=out_specs, check_vma=False)
```

```python
import functools

import jax
import jax.numpy as jnp
from jax import lax
from jax.experimental import pallas as pl
from jax.experimental.pallas import tpu as pltpu
from jax.sharding import PartitionSpec as P


F32 = jnp.float32
BF16 = jnp.bfloat16
VMEM = pl.BlockSpec(memory_space=pltpu.VMEM)
HBM = pl.BlockSpec(memory_space=pltpu.HBM)

S = 512
N = 64
M = 64
C = 32
Z = 128
T = 8
ROWS = N * T
EXTRA = 8


def column_of(row):
    n = row.shape[1]
    r = lax.broadcasted_iota(jnp.int32, (n, n), 0)
    c = lax.broadcasted_iota(jnp.int32, (n, n), 1)
    return jnp.sum(jnp.where(r == c, jnp.broadcast_to(row, (n, n)), 0.0), axis=1, keepdims=True)


def normalize(x, gain, bias):
    values = x.astype(F32)
    center = values - jnp.mean(values, axis=1, keepdims=True)
    spread = jnp.mean(center * center, axis=1, keepdims=True)
    return center * lax.rsqrt(spread + 1e-05) * gain[None] + bias[None]


def tokens_of(tok_ref, start, count):
    token = tok_ref[...].astype(F32)
    t_iota = lax.broadcasted_iota(jnp.int32, (count, N), 0)
    l_iota = lax.broadcasted_iota(jnp.int32, (count, N), 1)
    return jnp.sum(
        jnp.where(l_iota == t_iota + start, jnp.broadcast_to(token, (count, N)), 0.0), axis=1, keepdims=True
    )


def pack_kernel(wl_ref, wo_ref, out_ref):
    out_ref[0:Z, :] = wo_ref[...]
    out_ref[Z : Z + 16, :] = jnp.zeros((16, Z), BF16)
    out_ref[Z : Z + 4, 0:M] = wl_ref[...]


def stack_kernel(a, b, c, d, out):
    for i, ref in enumerate((a, b, c, d)):
        out[i] = ref[...]


def weight_kernel(near, far, wl_out, w2_out):
    packs = [near[i] for i in range(4)] + [far[i] for i in range(4)]
    for i in range(0, 8, 2):
        a, b = (packs[i + j][:Z, :].astype(F32).T.astype(BF16) for j in range(2))
        w2_out[:Z, i * 64 : i * 64 + 128] = jnp.concatenate([a[:, :64], b[:, :64]], axis=1)
        w2_out[Z:, i * 64 : i * 64 + 128] = jnp.concatenate([a[:, 64:], b[:, 64:]], axis=1)
    lefts = jnp.concatenate([pack[Z:, :M] for pack in packs], axis=0)
    r = lax.broadcasted_iota(jnp.int32, (C, 128), 0)
    c = lax.broadcasted_iota(jnp.int32, (C, 128), 1)
    pick = c == r // 4 * 16 + r % 2 * 2 + r // 2 % 2
    wl_out[...] = jnp.dot(pick.astype(F32).astype(BF16), lefts, preferred_element_type=F32).astype(BF16)


def right_kernel(x_ref, row_hbm, tok_hbm, gain_hbm, bias_hbm, wr_hbm, out_ref, buf, row_ref, tok_ref, gain_ref, bias_ref, wr_ref, sems):
    k = lax.axis_index("chan")
    pieces = (
        (x_ref.at[pl.ds(k * T, T)], buf),
        (gain_hbm, gain_ref),
        (bias_hbm, bias_ref),
        (tok_hbm, tok_ref),
        (row_hbm, row_ref),
        (wr_hbm, wr_ref),
    )
    copies = [pltpu.make_async_copy(src, dst, sems.at[i]) for i, (src, dst) in enumerate(pieces)]
    for copy in copies:
        copy.start()
    for copy in copies[1:]:
        copy.wait()
    gain = column_of(gain_ref[...])
    bias = column_of(bias_ref[...])
    token_col = tokens_of(tok_ref, k * T, T)
    weight = token_col * row_ref[...].astype(F32)
    wr = wr_ref[...]
    pad = jnp.concatenate([jnp.broadcast_to(token_col, (T, S)), jnp.zeros((T, S), F32)], axis=0)
    out_ref[T * C :, :] = pad.astype(BF16)
    copies[0].wait()
    for t in range(T):
        normed = normalize(buf[t : t + 1], gain, bias).astype(BF16)
        part = jnp.dot(wr, normed[0], preferred_element_type=F32)
        out_ref[t * C : (t + 1) * C, :] = (part * weight[t : t + 1]).astype(BF16)


def norm_kernel(half, x_ref, gain_ref, bias_ref, out_ref, buf, sems):
    copies = [
        pltpu.make_async_copy(x_ref.at[pl.ds(half * N // 2 + g * T, T)], buf.at[g], sems.at[g])
        for g in range(N // 2 // T)
    ]
    for copy in copies:
        copy.start()
    gain = column_of(gain_ref[...])
    bias = column_of(bias_ref[...])
    for g, copy in enumerate(copies):
        copy.wait()

        def one(t, carry):
            normed = normalize(buf[g, pl.ds(t, 1)], gain, bias)
            out_ref[pl.ds(pl.multiple_of((g * T + t) * M, M), M), :] = normed[0].astype(BF16)
            return carry

        lax.fori_loop(0, T, one, 0, unroll=4)


def left_kernel(n_a, n_b, wl_ref, row_ref, tok_ref, out_ref):
    rep = (
        lax.broadcasted_iota(jnp.int32, (C * T, C), 0) // T == lax.broadcasted_iota(jnp.int32, (C * T, C), 1)
    ).astype(F32).astype(BF16)
    tile = (
        lax.broadcasted_iota(jnp.int32, (M, T * M), 0) == lax.broadcasted_iota(jnp.int32, (M, T * M), 1) % M
    ).astype(F32).astype(BF16)
    tall = jnp.dot(rep, wl_ref[...], preferred_element_type=F32).astype(BF16)
    full = jnp.dot(tall, tile, preferred_element_type=F32)
    own = (
        lax.broadcasted_iota(jnp.int32, (C * T, T * M), 0) % T
        == lax.broadcasted_iota(jnp.int32, (C * T, T * M), 1) // M
    )
    wide = jnp.where(own, full, 0.0).astype(BF16)
    rows = row_ref[...].astype(F32)
    for g in range(N // T):
        weight = tokens_of(tok_ref, g * T, T) * rows
        n_ref, at = (n_a, g) if g < N // T // 2 else (n_b, g - N // T // 2)
        part = jnp.dot(wide, n_ref[at * T * M : (at + 1) * T * M, :], preferred_element_type=F32)
        out_ref[:, g * T : (g + 1) * T, :] = (part.reshape(C, T, S) * weight[None]).astype(BF16)


def pair_blocks(blocks, lf_ref, w2_ref, row_ref, spread):
    rhs = jnp.concatenate([rows for rows, _, _ in blocks], axis=0) if len(blocks) > 1 else blocks[0][0]
    for n in range(8):
        part = lax.dot_general(
            rhs, lf_ref[n * 256 : (n + 1) * 256, :], (((1,), (1,)), ((), ())), preferred_element_type=F32
        ).astype(BF16)
        for b in range(len(blocks)):
            for t in range(T):
                for u in range(2):
                    hi = n * 2 + u
                    spread[b * T // 2 + t // 2, hi * C : (hi + 1) * C, (t % 2) * 128 : (t % 2) * 128 + 128] = part[
                        (b * T + t) * C : (b * T + t + 1) * C, u * 128 : (u + 1) * 128
                    ]
    low = lax.broadcasted_iota(jnp.int32, (Z, 128), 1) < N
    rows_used = jnp.sum(row_ref[...].astype(F32), axis=1, keepdims=True)
    lane = lax.broadcasted_iota(jnp.int32, (EXTRA, Z), 1)
    w2 = w2_ref[...]
    for b, (_, extra, store) in enumerate(blocks):
        for p in range(T // 2):
            both = jnp.dot(w2, spread[b * T // 2 + p], preferred_element_type=F32)
            x0, y0 = both[:Z, :128], both[Z:, :128]
            x1, y1 = both[:Z, 128:], both[Z:, 128:]
            pair = jnp.where(low, x0, y1) + pltpu.roll(jnp.where(low, x1, y0), N, 1)
            flat = pair.T
            store(pl.ds(2 * p, N, stride=T), flat[:N])
            store(pl.ds(2 * p + 1, N, stride=T), flat[N:])
        mask = jnp.broadcast_to(extra.astype(F32)[:EXTRA, :1], (EXTRA, Z))
        store(pl.ds(ROWS, EXTRA), jnp.where(lane < N, jnp.broadcast_to(rows_used, (EXTRA, Z)), mask))


def whole(ref):
    return ref[: T * C, :], ref[T * C :, :]


def halves(first, second):
    return jnp.concatenate([first[...], second[:128, :]], axis=0), second[128:, :]


def to(ref):
    def store(where, value):
        ref[where, :] = value

    return store


def half_of(ref, b):
    return to(ref.at[b])


def choose(first, a, b, one, two):
    one[...] = jnp.where(first, a, b)
    two[...] = jnp.where(first, b, a)


def core():
    return lax.rem(lax.axis_index("col"), 2)


def first_kernel(own, lf, w2, row, out, spread):
    pair_blocks([whole(own) + (to(out),)], lf, w2, row, spread)


def two_kernel(back, ahead, lf, w2, row, keep, send, spread, both):
    pair_blocks([whole(back) + (half_of(both, 0),), whole(ahead) + (half_of(both, 1),)], lf, w2, row, spread)
    choose(core() == 0, both[1], both[0], keep, send)


def mixed_kernel(back, ahead, base, lf, w2, row, keep, send, rest, spread, both):
    pair_blocks([whole(back) + (to(rest),), whole(ahead) + (half_of(both, 0),)], lf, w2, row, spread)
    choose(core() == 0, base[...], both[0], keep, send)


def last_kernel(first, second, rest, lf, w2, row, keep, send, spread, both):
    pair_blocks([halves(first, second) + (half_of(both, 0),)], lf, w2, row, spread)
    choose(core() == 0, both[0], rest[...], keep, send)


def add_kernel(swapped, keep_a, got_a, keep_b, got_b, keep, send):
    a = keep_a[...] + got_a[...]
    b = keep_b[...] + got_b[...]
    first = lax.axis_index("col") // 2 == 0
    if swapped:
        first = lax.axis_index("col") // 2 == core()
    choose(first, a, b, keep, send)


def final_kernel(keep, got, tok_ref, bias_ref, out):
    total = keep[...] + got[...]
    tail = total[ROWS:, :]
    rows_used = tail[0:1, 0:1]
    second = (tail[:, N : N + 1] > 0.0).astype(F32)
    first = column_of(tok_ref[...].astype(F32))
    count = jnp.maximum(rows_used[None] * first[:, :, None] * second[None], 1.0)
    pairs = total[:ROWS, :].reshape(N, T, Z)
    out[...] = ((pairs + bias_ref[...][None]) / count).astype(BF16)


def call(kernel, out, *args, specs=None, scratch=(), flops=0, limit=10):
    leaves = jax.tree.leaves(out)
    bytes_accessed = sum(a.size * a.dtype.itemsize for a in list(args) + leaves)
    return pl.pallas_call(
        kernel,
        out_shape=out,
        in_specs=specs or [VMEM] * len(args),
        out_specs=jax.tree.map(lambda _: VMEM, out),
        scratch_shapes=scratch,
        compiler_params=pltpu.CompilerParams(vmem_limit_bytes=limit << 20),
        cost_estimate=pl.CostEstimate(flops=flops, bytes_accessed=bytes_accessed, transcendentals=0),
    )(*args)


def in_hbm(value):
    return pltpu.with_memory_space_constraint(value, pltpu.HBM)


def shape(dims, dtype):
    return jax.ShapeDtypeStruct(dims, dtype)


def program(x, row_mask, token_mask, gain, bias, wl, wr, wo, out_bias):
    xt = in_hbm(x.transpose(1, 2, 0))
    row = row_mask.reshape(1, S)
    tok = token_mask.reshape(1, N)
    gain, bias = gain.reshape(1, M), bias.reshape(1, M)

    ring = [[(i, (i + d) % 8) for i in range(8)] for d in (1, -1)]
    y_ring = {d: [(a * 4 + b, a * 4 + (b + d) % 4) for a in range(2) for b in range(4)] for d in (1, -1, 2)}
    x_swap = [(c, (c + 4) % 8) for c in range(8)]
    core_swap = [(0, 1), (1, 0), (2, 3), (3, 2)]
    xh_swap = [(0, 2), (1, 3), (2, 0), (3, 1)]

    pack = call(pack_kernel, shape((Z + 16, Z), BF16), wl.T, wo)
    up = lax.ppermute(pack, "chan", y_ring[1])
    down = lax.ppermute(pack, "chan", y_ring[-1])
    over = lax.ppermute(pack, "chan", y_ring[2])
    four = call(stack_kernel, shape((4, Z + 16, Z), BF16), pack, up, down, over, limit=4)
    other = lax.ppermute(four, "chan", x_swap)
    wl_all, w2 = call(weight_kernel, (shape((C, M), BF16), shape((2 * Z, 512), BF16)), four, other, limit=4)

    small = [in_hbm(a) for a in (row, tok, gain, bias, wr.T)]
    own = call(
        right_kernel, shape((T * C + 16, S), BF16), xt, *small,
        specs=[HBM] * 6,
        scratch=[pltpu.VMEM((T, M, S), BF16)] + [pltpu.VMEM(a.shape, a.dtype) for a in small] + [pltpu.SemaphoreType.DMA((6,))],
        flops=20 << 20, limit=8,
    )

    ahead, back = own, own
    from_back, from_ahead = [], []
    for _ in range(3):
        back = lax.ppermute(back, "row", ring[0])
        ahead = lax.ppermute(ahead, "row", ring[1])
        from_back.append(back)
        from_ahead.append(ahead)
    half_a = lax.ppermute(back[:128], "row", ring[0])
    half_b = lax.ppermute(ahead[128:], "row", ring[1])

    normed = [
        call(
            functools.partial(norm_kernel, half), shape((N * M // 2, S), BF16), xt, gain, bias,
            specs=[HBM, VMEM, VMEM],
            scratch=[pltpu.VMEM((N // 2 // T, T, M, S), BF16), pltpu.SemaphoreType.DMA((N // 2 // T,))],
            flops=15 << 20, limit=8,
        )
        for half in range(2)
    ]
    left = call(left_kernel, shape((C, N, S), BF16), *normed, wl_all, row, tok, flops=1 << 30, limit=8)
    lf = left.reshape(C * N, S)

    block = shape((ROWS + EXTRA, Z), F32)
    pair = (block, block)
    one = 800 << 20
    shared = (lf, w2, row)

    def spread(n):
        return [pltpu.VMEM((n * T // 2, 512, 256), BF16), pltpu.VMEM((n, ROWS + EXTRA, Z), F32)]

    p0 = call(first_kernel, block, own, *shared, scratch=spread(1)[:1], flops=one)
    k1, s1 = call(two_kernel, pair, from_back[0], from_ahead[0], *shared, scratch=spread(2), flops=2 * one)
    k2, s2, rest = call(mixed_kernel, (block,) * 3, from_back[1], from_ahead[1], p0, *shared, scratch=spread(2), flops=2 * one)
    k3, s3 = call(two_kernel, pair, from_back[2], from_ahead[2], *shared, scratch=spread(2), flops=2 * one)
    k4, s4 = call(last_kernel, pair, half_a, half_b, rest, *shared, scratch=spread(1), flops=one)

    e1 = lax.ppermute(s1, "col", core_swap)
    e2 = lax.ppermute(s2, "col", core_swap)
    e3 = lax.ppermute(s3, "col", core_swap)
    e4 = lax.ppermute(s4, "col", core_swap)
    odd, odd_sent = call(functools.partial(add_kernel, True), pair, k1, e1, k3, e3)
    f1 = lax.ppermute(odd_sent, "col", xh_swap)
    even, even_sent = call(functools.partial(add_kernel, False), pair, k2, e2, k4, e4)
    f2 = lax.ppermute(even_sent, "col", xh_swap)
    part = shape((N, T, Z), BF16)
    out_bias = out_bias.reshape(1, Z)
    y1 = call(final_kernel, part, odd, f1, tok, out_bias)
    y2 = call(final_kernel, part, even, f2, tok, out_bias)

    def home(kept):
        return [(z * 4 + c, (z + kept[c]) % 8 * 4 + z // 2) for z in range(8) for c in range(4)]

    g1 = lax.ppermute(y1, ("row", "col"), home((1, -3, 3, -1)))
    g2 = lax.ppermute(y2, ("row", "col"), home((0, 2, 4, -2)))
    low_row = lax.axis_index("row") % 2 == 0
    return jnp.where(low_row, jnp.concatenate([g2, g1], 0), jnp.concatenate([g1, g2], 0))


def solution(mesh):
    in_specs = (
        P("col", "row", None),
        P("col"),
        P("row"),
        P(),
        P(),
        P(None, "chan"),
        P(),
        P("chan", None),
        P(),
    )
    out_specs = P("col", ("row", "chan"), None)
    return jax.shard_map(program, mesh=mesh, in_specs=in_specs, out_specs=out_specs, check_vma=False)
```

```python
import functools

import jax
import jax.numpy as jnp
from jax import lax
from jax.experimental import pallas as pl
from jax.experimental.pallas import tpu as pltpu
from jax.sharding import PartitionSpec as P


F32 = jnp.float32
BF16 = jnp.bfloat16
VMEM = pl.BlockSpec(memory_space=pltpu.VMEM)
HBM = pl.BlockSpec(memory_space=pltpu.HBM)

S = 512
N = 64
M = 64
C = 32
Z = 128
T = 8
ROWS = N * T
EXTRA = 8


def column_of(row):
    n = row.shape[1]
    r = lax.broadcasted_iota(jnp.int32, (n, n), 0)
    c = lax.broadcasted_iota(jnp.int32, (n, n), 1)
    return jnp.sum(jnp.where(r == c, jnp.broadcast_to(row, (n, n)), 0.0), axis=1, keepdims=True)


def normalize(x, gain, bias):
    values = x.astype(F32)
    center = values - jnp.mean(values, axis=1, keepdims=True)
    spread = jnp.mean(center * center, axis=1, keepdims=True)
    return center * lax.rsqrt(spread + 1e-05) * gain[None] + bias[None]


def tokens_of(tok_ref, start, count):
    token = tok_ref[...].astype(F32)
    t_iota = lax.broadcasted_iota(jnp.int32, (count, N), 0)
    l_iota = lax.broadcasted_iota(jnp.int32, (count, N), 1)
    return jnp.sum(
        jnp.where(l_iota == t_iota + start, jnp.broadcast_to(token, (count, N)), 0.0), axis=1, keepdims=True
    )


def pack_kernel(wl_ref, wo_ref, out_ref):
    out_ref[0:Z, :] = wo_ref[...]
    out_ref[Z : Z + 16, :] = jnp.zeros((16, Z), BF16)
    out_ref[Z : Z + 4, 0:M] = wl_ref[...]


def stack_kernel(a, b, c, d, out):
    for i, ref in enumerate((a, b, c, d)):
        out[i] = ref[...]


def weight_kernel(near, far, wl_out, w2_out):
    packs = [near[i] for i in range(4)] + [far[i] for i in range(4)]
    for i in range(0, 8, 2):
        a, b = (packs[i + j][:Z, :].astype(F32).T.astype(BF16) for j in range(2))
        w2_out[:Z, i * 64 : i * 64 + 128] = jnp.concatenate([a[:, :64], b[:, :64]], axis=1)
        w2_out[Z:, i * 64 : i * 64 + 128] = jnp.concatenate([a[:, 64:], b[:, 64:]], axis=1)
    lefts = jnp.concatenate([pack[Z:, :M] for pack in packs], axis=0)
    r = lax.broadcasted_iota(jnp.int32, (C, 128), 0)
    c = lax.broadcasted_iota(jnp.int32, (C, 128), 1)
    pick = c == r // 4 * 16 + r % 2 * 2 + r // 2 % 2
    wl_out[...] = jnp.dot(pick.astype(F32).astype(BF16), lefts, preferred_element_type=F32).astype(BF16)


def right_kernel(x_ref, row_hbm, tok_hbm, gain_hbm, bias_hbm, wr_hbm, out_ref, buf, row_ref, tok_ref, gain_ref, bias_ref, wr_ref, sems):
    k = lax.axis_index("chan")
    pieces = (
        (x_ref.at[pl.ds(k * T, T)], buf),
        (gain_hbm, gain_ref),
        (bias_hbm, bias_ref),
        (tok_hbm, tok_ref),
        (row_hbm, row_ref),
        (wr_hbm, wr_ref),
    )
    copies = [pltpu.make_async_copy(src, dst, sems.at[i]) for i, (src, dst) in enumerate(pieces)]
    for copy in copies:
        copy.start()
    for copy in copies[1:]:
        copy.wait()
    gain = column_of(gain_ref[...])
    bias = column_of(bias_ref[...])
    token_col = tokens_of(tok_ref, k * T, T)
    weight = token_col * row_ref[...].astype(F32)
    wr = wr_ref[...]
    rows = row_ref[...].astype(F32)
    pad = jnp.concatenate([jnp.broadcast_to(token_col, (T, S)), rows, jnp.zeros((T - 1, S), F32)], axis=0)
    out_ref[T * C :, :] = pad.astype(BF16)
    copies[0].wait()
    for t in range(T):
        normed = normalize(buf[t : t + 1], gain, bias).astype(BF16)
        part = jnp.dot(wr, normed[0], preferred_element_type=F32)
        out_ref[t * C : (t + 1) * C, :] = (part * weight[t : t + 1]).astype(BF16)


def norm_kernel(half, x_ref, gain_ref, bias_ref, out_ref, buf, sems):
    copies = [
        pltpu.make_async_copy(x_ref.at[pl.ds(half * N // 2 + g * T, T)], buf.at[g], sems.at[g])
        for g in range(N // 2 // T)
    ]
    for copy in copies:
        copy.start()
    gain = column_of(gain_ref[...])
    bias = column_of(bias_ref[...])
    for g, copy in enumerate(copies):
        copy.wait()

        def one(t, carry):
            normed = normalize(buf[g, pl.ds(t, 1)], gain, bias)
            out_ref[pl.ds(pl.multiple_of((g * T + t) * M, M), M), :] = normed[0].astype(BF16)
            return carry

        lax.fori_loop(0, T, one, 0, unroll=4)


def left_kernel(n_a, n_b, wl_ref, row_ref, tok_ref, out_ref):
    rep = (
        lax.broadcasted_iota(jnp.int32, (C * T, C), 0) // T == lax.broadcasted_iota(jnp.int32, (C * T, C), 1)
    ).astype(F32).astype(BF16)
    tile = (
        lax.broadcasted_iota(jnp.int32, (M, T * M), 0) == lax.broadcasted_iota(jnp.int32, (M, T * M), 1) % M
    ).astype(F32).astype(BF16)
    tall = jnp.dot(rep, wl_ref[...], preferred_element_type=F32).astype(BF16)
    full = jnp.dot(tall, tile, preferred_element_type=F32)
    own = (
        lax.broadcasted_iota(jnp.int32, (C * T, T * M), 0) % T
        == lax.broadcasted_iota(jnp.int32, (C * T, T * M), 1) // M
    )
    wide = jnp.where(own, full, 0.0).astype(BF16)
    rows = row_ref[...].astype(F32)
    for g in range(N // T):
        weight = tokens_of(tok_ref, g * T, T) * rows
        n_ref, at = (n_a, g) if g < N // T // 2 else (n_b, g - N // T // 2)
        part = jnp.dot(wide, n_ref[at * T * M : (at + 1) * T * M, :], preferred_element_type=F32)
        out_ref[:, g * T : (g + 1) * T, :] = (part.reshape(C, T, S) * weight[None]).astype(BF16)


def join_kernel(own, got, out):
    half = T * C
    out[:half, :] = own[:half, :]
    out[half : 2 * half, :] = got[:half, :]
    mine, other = own[half:, :].astype(F32), got[half:, :].astype(F32)
    pad = jnp.concatenate([mine[: T + 1], other[T : T + 1], jnp.zeros((T - 2, S), F32)], axis=0)
    out[2 * half :, :] = pad.astype(BF16)


def pair_block(right, lf_own, lf_got, w2_ref, spread, out):
    half = T * C
    for n in range(8):
        part = sum(
            lax.dot_general(
                right[b * half : (b + 1) * half, :],
                lf[n * 256 : (n + 1) * 256, :],
                (((1,), (1,)), ((), ())),
                preferred_element_type=F32,
            )
            for b, lf in enumerate((lf_own, lf_got))
        ).astype(BF16)
        for t in range(T):
            for u in range(2):
                hi = n * 2 + u
                spread[t // 2, hi * C : (hi + 1) * C, (t % 2) * 128 : (t % 2) * 128 + 128] = part[
                    t * C : (t + 1) * C, u * 128 : (u + 1) * 128
                ]
    low = lax.broadcasted_iota(jnp.int32, (Z, 128), 1) < N
    w2 = w2_ref[...]
    for p in range(T // 2):
        both = jnp.dot(w2, spread[p], preferred_element_type=F32)
        x0, y0 = both[:Z, :128], both[Z:, :128]
        x1, y1 = both[:Z, 128:], both[Z:, 128:]
        pair = jnp.where(low, x0, y1) + pltpu.roll(jnp.where(low, x1, y0), N, 1)
        out[p * 128 : (p + 1) * 128, :] = pair.T
    extra = right[2 * half :, :].astype(F32)
    counts = jnp.sum(extra[T : T + 2], axis=1, keepdims=True)
    rows_used = jnp.broadcast_to(counts[0:1] + counts[1:2], (EXTRA, Z))
    lane = lax.broadcasted_iota(jnp.int32, (EXTRA, Z), 1)
    out[ROWS:, :] = jnp.where(lane < N, rows_used, jnp.broadcast_to(extra[:EXTRA, :1], (EXTRA, Z)))


def choose(first, a, b, one, two):
    one[...] = jnp.where(first, a, b)
    two[...] = jnp.where(first, b, a)


def core():
    return lax.rem(lax.axis_index("col"), 2)


def x_half():
    return lax.axis_index("col") // 2


def first_kernel(right, lf_own, lf_got, w2, out, spread):
    @pl.when(core() == 0)
    def _():
        pair_block(right, lf_own, lf_got, w2, spread, out)


def next_kernel(right, lf_own, lf_got, w2, out, spread):
    pair_block(right, lf_own, lf_got, w2, spread, out)


def odd_kernel(right, one, lf_own, lf_got, w2, keep, send, spread, three):
    pair_block(right, lf_own, lf_got, w2, spread, three)
    choose(x_half() == 0, one[...], three[...], keep, send)


def even_kernel(right, zero, two, lf_own, lf_got, w2, keep, send, spread, last):
    @pl.when(core() == 1)
    def _():
        pair_block(right, lf_own, lf_got, w2, spread, last)

    @pl.when(core() == 0)
    def _():
        last[...] = zero[...]

    choose(x_half() == 0, two[...], last[...], keep, send)


def final_kernel(keep, got, tok_ref, bias_ref, out):
    total = keep[...] + got[...]
    tail = total[ROWS:, :]
    rows_used = tail[0:1, 0:1]
    second = (tail[:, N : N + 1] > 0.0).astype(F32)
    first = column_of(tok_ref[...].astype(F32))
    count = jnp.maximum(rows_used[None] * first[None] * second[:, :, None], 1.0)
    pairs = total[:ROWS, :].reshape(T, N, Z)
    out[...] = ((pairs + bias_ref[...][None]) / count).reshape(ROWS, Z).astype(BF16)


def assemble_kernel(odd, even, out, flat):
    low = lax.rem(lax.axis_index("row"), 2) == 0
    a, b = odd[...].astype(F32), even[...].astype(F32)
    for h, rows in enumerate((jnp.where(low, b, a), jnp.where(low, a, b))):
        for t in range(T):
            flat[h, pl.ds(t, N, stride=T), :] = rows[t * N : (t + 1) * N]
        out[h * N : (h + 1) * N] = flat[h].reshape(N, T, Z).astype(BF16)


def call(kernel, out, *args, specs=None, scratch=(), flops=0, limit=10):
    leaves = jax.tree.leaves(out)
    bytes_accessed = sum(a.size * a.dtype.itemsize for a in list(args) + leaves)
    return pl.pallas_call(
        kernel,
        out_shape=out,
        in_specs=specs or [VMEM] * len(args),
        out_specs=jax.tree.map(lambda _: VMEM, out),
        scratch_shapes=scratch,
        compiler_params=pltpu.CompilerParams(vmem_limit_bytes=limit << 20),
        cost_estimate=pl.CostEstimate(flops=flops, bytes_accessed=bytes_accessed, transcendentals=0),
    )(*args)


def in_hbm(value):
    return pltpu.with_memory_space_constraint(value, pltpu.HBM)


def shape(dims, dtype):
    return jax.ShapeDtypeStruct(dims, dtype)


def program(x, row_mask, token_mask, gain, bias, wl, wr, wo, out_bias):
    xt = in_hbm(x.transpose(1, 2, 0))
    row = row_mask.reshape(1, S)
    tok = token_mask.reshape(1, N)
    gain, bias = gain.reshape(1, M), bias.reshape(1, M)

    y_ring = {d: [(a * 4 + b, a * 4 + (b + d) % 4) for a in range(2) for b in range(4)] for d in (1, -1, 2)}
    x_swap = [(c, (c + 4) % 8) for c in range(8)]
    core_swap = [(0, 1), (1, 0), (2, 3), (3, 2)]
    xh_swap = [(0, 2), (1, 3), (2, 0), (3, 1)]

    pack = call(pack_kernel, shape((Z + 16, Z), BF16), wl.T, wo)
    up = lax.ppermute(pack, "chan", y_ring[1])
    down = lax.ppermute(pack, "chan", y_ring[-1])
    over = lax.ppermute(pack, "chan", y_ring[2])
    four = call(stack_kernel, shape((4, Z + 16, Z), BF16), pack, up, down, over, limit=4)
    other = lax.ppermute(four, "chan", x_swap)
    wl_all, w2 = call(weight_kernel, (shape((C, M), BF16), shape((2 * Z, 512), BF16)), four, other, limit=4)

    small = [in_hbm(a) for a in (row, tok, gain, bias, wr.T)]
    own = call(
        right_kernel, shape((T * C + 16, S), BF16), xt, *small,
        specs=[HBM] * 6,
        scratch=[pltpu.VMEM((T, M, S), BF16)] + [pltpu.VMEM(a.shape, a.dtype) for a in small] + [pltpu.SemaphoreType.DMA((6,))],
        flops=20 << 20, limit=8,
    )

    got = lax.ppermute(own, "col", core_swap)
    right = [call(join_kernel, shape((2 * T * C + 16, S), BF16), own, got, limit=4)]

    for step in range(4):
        pairs = [(z * 4 + c, (z + 1 - 2 * (c % 2)) % 8 * 4 + c) for z in range(8) for c in range(4) if step < 3 or c % 2]
        right.append(lax.ppermute(right[-1], ("row", "col"), pairs))

    normed = [
        call(
            functools.partial(norm_kernel, half), shape((N * M // 2, S), BF16), xt, gain, bias,
            specs=[HBM, VMEM, VMEM],
            scratch=[pltpu.VMEM((N // 2 // T, T, M, S), BF16), pltpu.SemaphoreType.DMA((N // 2 // T,))],
            flops=15 << 20, limit=8,
        )
        for half in range(2)
    ]
    left = call(left_kernel, shape((C, N, S), BF16), *normed, wl_all, row, tok, flops=1 << 30, limit=8)
    lf = left.reshape(C * N, S)
    lf_got = lax.ppermute(lf, "col", core_swap)

    block = shape((ROWS + EXTRA, Z), F32)
    one = 1400 << 20
    shared = (lf, lf_got, w2)
    spread = [pltpu.VMEM((T // 2, 512, 256), BF16)]
    more = spread + [pltpu.VMEM((ROWS + EXTRA, Z), F32)]
    p0 = call(first_kernel, block, right[0], *shared, scratch=spread, flops=one)
    p1 = call(next_kernel, block, right[1], *shared, scratch=spread, flops=one)
    p2 = call(next_kernel, block, right[2], *shared, scratch=spread, flops=one)
    odd, odd_sent = call(odd_kernel, (block,) * 2, right[3], p1, *shared, scratch=more, flops=one)
    f1 = lax.ppermute(odd_sent, "col", xh_swap)
    even, even_sent = call(even_kernel, (block,) * 2, right[4], p0, p2, *shared, scratch=more, flops=one)
    f2 = lax.ppermute(even_sent, "col", xh_swap)
    part = shape((ROWS, Z), BF16)
    out_bias = out_bias.reshape(1, Z)
    y1 = call(final_kernel, part, odd, f1, tok, out_bias)
    y2 = call(final_kernel, part, even, f2, tok, out_bias)

    def home(kept):
        return [(z * 4 + c, (z + kept[c]) % 8 * 4 + z // 2) for z in range(8) for c in range(4)]

    g1 = lax.ppermute(y1, ("row", "col"), home((-1, 1, -3, 3)))
    g2 = lax.ppermute(y2, ("row", "col"), home((-2, 2, 0, 4)))
    return call(assemble_kernel, shape((2 * N, T, Z), BF16), g1, g2, scratch=[pltpu.VMEM((2, ROWS, Z), F32)], limit=4)


def solution(mesh):
    in_specs = (
        P("col", "row", None),
        P("col"),
        P("row"),
        P(),
        P(),
        P(None, "chan"),
        P(),
        P("chan", None),
        P(),
    )
    out_specs = P("col", ("row", "chan"), None)
    return jax.shard_map(program, mesh=mesh, in_specs=in_specs, out_specs=out_specs, check_vma=False)
```

```python
import functools

import jax
import jax.numpy as jnp
from jax import lax
from jax.experimental import pallas as pl
from jax.experimental.pallas import tpu as pltpu
from jax.sharding import PartitionSpec as P


F32 = jnp.float32
BF16 = jnp.bfloat16
VMEM = pl.BlockSpec(memory_space=pltpu.VMEM)
HBM = pl.BlockSpec(memory_space=pltpu.HBM)

S = 512
N = 64
M = 64
C = 32
Z = 128
T = 8
ROWS = N * T
EXTRA = 8


def column_of(row):
    n = row.shape[1]
    r = lax.broadcasted_iota(jnp.int32, (n, n), 0)
    c = lax.broadcasted_iota(jnp.int32, (n, n), 1)
    return jnp.sum(jnp.where(r == c, jnp.broadcast_to(row, (n, n)), 0.0), axis=1, keepdims=True)


def normalize(x, gain, bias):
    values = x.astype(F32)
    center = values - jnp.mean(values, axis=1, keepdims=True)
    spread = jnp.mean(center * center, axis=1, keepdims=True)
    return center * lax.rsqrt(spread + 1e-05) * gain[None] + bias[None]


def tokens_of(tok_ref, start, count):
    token = tok_ref[...].astype(F32)
    t_iota = lax.broadcasted_iota(jnp.int32, (count, N), 0)
    l_iota = lax.broadcasted_iota(jnp.int32, (count, N), 1)
    return jnp.sum(
        jnp.where(l_iota == t_iota + start, jnp.broadcast_to(token, (count, N)), 0.0), axis=1, keepdims=True
    )


def pack_kernel(wl_ref, wo_ref, out_ref):
    out_ref[0:Z, :] = wo_ref[...]
    out_ref[Z : Z + 16, :] = jnp.zeros((16, Z), BF16)
    out_ref[Z : Z + 4, 0:M] = wl_ref[...]


def stack_kernel(a, b, c, d, out):
    for i, ref in enumerate((a, b, c, d)):
        out[i] = ref[...]


def weight_kernel(near, far, wl_out, w2_out):
    packs = [near[i] for i in range(4)] + [far[i] for i in range(4)]
    for i in range(0, 8, 2):
        a, b = (packs[i + j][:Z, :].astype(F32).T.astype(BF16) for j in range(2))
        w2_out[:Z, i * 64 : i * 64 + 128] = jnp.concatenate([a[:, :64], b[:, :64]], axis=1)
        w2_out[Z:, i * 64 : i * 64 + 128] = jnp.concatenate([a[:, 64:], b[:, 64:]], axis=1)
    lefts = jnp.concatenate([pack[Z:, :M] for pack in packs], axis=0)
    r = lax.broadcasted_iota(jnp.int32, (C, 128), 0)
    c = lax.broadcasted_iota(jnp.int32, (C, 128), 1)
    pick = c == r // 4 * 16 + r % 2 * 2 + r // 2 % 2
    wl_out[...] = jnp.dot(pick.astype(F32).astype(BF16), lefts, preferred_element_type=F32).astype(BF16)


def right_kernel(x_ref, row_hbm, tok_hbm, gain_hbm, bias_hbm, wr_hbm, out_ref, buf, row_ref, tok_ref, gain_ref, bias_ref, wr_ref, sems):
    k = lax.axis_index("chan")
    pieces = (
        (x_ref.at[pl.ds(k * T, T)], buf),
        (gain_hbm, gain_ref),
        (bias_hbm, bias_ref),
        (tok_hbm, tok_ref),
        (row_hbm, row_ref),
        (wr_hbm, wr_ref),
    )
    copies = [pltpu.make_async_copy(src, dst, sems.at[i]) for i, (src, dst) in enumerate(pieces)]
    for copy in copies:
        copy.start()
    for copy in copies[1:]:
        copy.wait()
    gain = column_of(gain_ref[...])
    bias = column_of(bias_ref[...])
    token_col = tokens_of(tok_ref, k * T, T)
    weight = token_col * row_ref[...].astype(F32)
    wr = wr_ref[...]
    rows = row_ref[...].astype(F32)
    pad = jnp.concatenate([jnp.broadcast_to(token_col, (T, S)), rows, jnp.zeros((T - 1, S), F32)], axis=0)
    out_ref[T * C :, :] = pad.astype(BF16)
    copies[0].wait()
    for t in range(T):
        normed = normalize(buf[t : t + 1], gain, bias).astype(BF16)
        part = jnp.dot(wr, normed[0], preferred_element_type=F32)
        out_ref[t * C : (t + 1) * C, :] = (part * weight[t : t + 1]).astype(BF16)


def norm_kernel(half, x_ref, gain_ref, bias_ref, out_ref, buf, sems):
    copies = [
        pltpu.make_async_copy(x_ref.at[pl.ds(half * N // 2 + g * T, T)], buf.at[g], sems.at[g])
        for g in range(N // 2 // T)
    ]
    for copy in copies:
        copy.start()
    gain = column_of(gain_ref[...])
    bias = column_of(bias_ref[...])
    for g, copy in enumerate(copies):
        copy.wait()

        def one(t, carry):
            normed = normalize(buf[g, pl.ds(t, 1)], gain, bias)
            out_ref[pl.ds(pl.multiple_of((g * T + t) * M, M), M), :] = normed[0].astype(BF16)
            return carry

        lax.fori_loop(0, T, one, 0, unroll=4)


def left_kernel(n_a, n_b, wl_ref, row_ref, tok_ref, out_ref):
    rep = (
        lax.broadcasted_iota(jnp.int32, (C * T, C), 0) // T == lax.broadcasted_iota(jnp.int32, (C * T, C), 1)
    ).astype(F32).astype(BF16)
    tile = (
        lax.broadcasted_iota(jnp.int32, (M, T * M), 0) == lax.broadcasted_iota(jnp.int32, (M, T * M), 1) % M
    ).astype(F32).astype(BF16)
    tall = jnp.dot(rep, wl_ref[...], preferred_element_type=F32).astype(BF16)
    full = jnp.dot(tall, tile, preferred_element_type=F32)
    own = (
        lax.broadcasted_iota(jnp.int32, (C * T, T * M), 0) % T
        == lax.broadcasted_iota(jnp.int32, (C * T, T * M), 1) // M
    )
    wide = jnp.where(own, full, 0.0).astype(BF16)
    rows = row_ref[...].astype(F32)
    for g in range(N // T):
        weight = tokens_of(tok_ref, g * T, T) * rows
        n_ref, at = (n_a, g) if g < N // T // 2 else (n_b, g - N // T // 2)
        part = jnp.dot(wide, n_ref[at * T * M : (at + 1) * T * M, :], preferred_element_type=F32)
        out_ref[:, g * T : (g + 1) * T, :] = (part.reshape(C, T, S) * weight[None]).astype(BF16)


def pair_block(right, other, lf_own, lf_got, w2_ref, spread, out):
    for n in range(8):
        part = sum(
            lax.dot_general(
                factor[: T * C, :],
                lf[n * 256 : (n + 1) * 256, :],
                (((1,), (1,)), ((), ())),
                preferred_element_type=F32,
            )
            for factor, lf in ((right, lf_own), (other, lf_got))
        ).astype(BF16)
        for t in range(T):
            for u in range(2):
                hi = n * 2 + u
                spread[t // 2, hi * C : (hi + 1) * C, (t % 2) * 128 : (t % 2) * 128 + 128] = part[
                    t * C : (t + 1) * C, u * 128 : (u + 1) * 128
                ]
    low = lax.broadcasted_iota(jnp.int32, (Z, 128), 1) < N
    w2 = w2_ref[...]
    for p in range(T // 2):
        both = jnp.dot(w2, spread[p], preferred_element_type=F32)
        x0, y0 = both[:Z, :128], both[Z:, :128]
        x1, y1 = both[:Z, 128:], both[Z:, 128:]
        pair = jnp.where(low, x0, y1) + pltpu.roll(jnp.where(low, x1, y0), N, 1)
        out[p * 128 : (p + 1) * 128, :] = pair.T
    extra = right[T * C :, :].astype(F32)
    rows = extra[T : T + 1] + other[T * C :, :].astype(F32)[T : T + 1]
    rows_used = jnp.broadcast_to(jnp.sum(rows, axis=1, keepdims=True), (EXTRA, Z))
    lane = lax.broadcasted_iota(jnp.int32, (EXTRA, Z), 1)
    out[ROWS:, :] = jnp.where(lane < N, rows_used, jnp.broadcast_to(extra[:EXTRA, :1], (EXTRA, Z)))


def choose(first, a, b, one, two):
    one[...] = jnp.where(first, a, b)
    two[...] = jnp.where(first, b, a)


def core():
    return lax.rem(lax.axis_index("col"), 2)


def x_half():
    return lax.axis_index("col") // 2


def first_kernel(right, other, lf_own, lf_got, w2, out, spread):
    @pl.when(core() == 0)
    def _():
        pair_block(right, other, lf_own, lf_got, w2, spread, out)


def next_kernel(right, other, lf_own, lf_got, w2, out, spread):
    pair_block(right, other, lf_own, lf_got, w2, spread, out)


def odd_kernel(right, other, one, lf_own, lf_got, w2, keep, send, spread, three):
    pair_block(right, other, lf_own, lf_got, w2, spread, three)
    choose(x_half() == 0, one[...], three[...], keep, send)


def even_kernel(right, other, zero, two, lf_own, lf_got, w2, keep, send, spread, last):
    @pl.when(core() == 1)
    def _():
        pair_block(right, other, lf_own, lf_got, w2, spread, last)

    @pl.when(core() == 0)
    def _():
        last[...] = zero[...]

    choose(x_half() == 0, two[...], last[...], keep, send)


def final_kernel(keep, got, tok_ref, bias_ref, out):
    total = keep[...] + got[...]
    tail = total[ROWS:, :]
    rows_used = tail[0:1, 0:1]
    second = (tail[:, N : N + 1] > 0.0).astype(F32)
    first = column_of(tok_ref[...].astype(F32))
    count = jnp.maximum(rows_used[None] * first[None] * second[:, :, None], 1.0)
    pairs = total[:ROWS, :].reshape(T, N, Z)
    out[...] = ((pairs + bias_ref[...][None]) / count).reshape(ROWS, Z).astype(BF16)


def assemble_kernel(odd, even, out, flat):
    low = lax.rem(lax.axis_index("row"), 2) == 0
    a, b = odd[...].astype(F32), even[...].astype(F32)
    for h, rows in enumerate((jnp.where(low, b, a), jnp.where(low, a, b))):
        for t in range(T):
            flat[h, pl.ds(t, N, stride=T), :] = rows[t * N : (t + 1) * N]
        out[h * N : (h + 1) * N] = flat[h].reshape(N, T, Z).astype(BF16)


def call(kernel, out, *args, specs=None, scratch=(), flops=0, limit=10):
    leaves = jax.tree.leaves(out)
    bytes_accessed = sum(a.size * a.dtype.itemsize for a in list(args) + leaves)
    return pl.pallas_call(
        kernel,
        out_shape=out,
        in_specs=specs or [VMEM] * len(args),
        out_specs=jax.tree.map(lambda _: VMEM, out),
        scratch_shapes=scratch,
        compiler_params=pltpu.CompilerParams(vmem_limit_bytes=limit << 20),
        cost_estimate=pl.CostEstimate(flops=flops, bytes_accessed=bytes_accessed, transcendentals=0),
    )(*args)


def in_hbm(value):
    return pltpu.with_memory_space_constraint(value, pltpu.HBM)


def shape(dims, dtype):
    return jax.ShapeDtypeStruct(dims, dtype)


def program(x, row_mask, token_mask, gain, bias, wl, wr, wo, out_bias):
    xt = in_hbm(x.transpose(1, 2, 0))
    row = row_mask.reshape(1, S)
    tok = token_mask.reshape(1, N)
    gain, bias = gain.reshape(1, M), bias.reshape(1, M)

    y_ring = {d: [(a * 4 + b, a * 4 + (b + d) % 4) for a in range(2) for b in range(4)] for d in (1, -1, 2)}
    x_swap = [(c, (c + 4) % 8) for c in range(8)]
    core_swap = [(0, 1), (1, 0), (2, 3), (3, 2)]
    xh_swap = [(0, 2), (1, 3), (2, 0), (3, 1)]

    pack = call(pack_kernel, shape((Z + 16, Z), BF16), wl.T, wo)
    up = lax.ppermute(pack, "chan", y_ring[1])
    down = lax.ppermute(pack, "chan", y_ring[-1])
    over = lax.ppermute(pack, "chan", y_ring[2])
    four = call(stack_kernel, shape((4, Z + 16, Z), BF16), pack, up, down, over, limit=4)
    other = lax.ppermute(four, "chan", x_swap)
    wl_all, w2 = call(weight_kernel, (shape((C, M), BF16), shape((2 * Z, 512), BF16)), four, other, limit=4)

    small = [in_hbm(a) for a in (row, tok, gain, bias, wr.T)]
    own = call(
        right_kernel, shape((T * C + 16, S), BF16), xt, *small,
        specs=[HBM] * 6,
        scratch=[pltpu.VMEM((T, M, S), BF16)] + [pltpu.VMEM(a.shape, a.dtype) for a in small] + [pltpu.SemaphoreType.DMA((6,))],
        flops=20 << 20, limit=8,
    )

    chains = [own, lax.ppermute(own, "col", core_swap)]
    right = [chains]
    for step in range(4):
        pairs = [(z * 4 + c, (z + 1 - 2 * (c % 2)) % 8 * 4 + c) for z in range(8) for c in range(4) if step < 3 or c % 2]
        chains = [lax.ppermute(chains[i], ("row", "col"), pairs) for i in range(2)]
        right.append(chains)

    normed = [
        call(
            functools.partial(norm_kernel, half), shape((N * M // 2, S), BF16), xt, gain, bias,
            specs=[HBM, VMEM, VMEM],
            scratch=[pltpu.VMEM((N // 2 // T, T, M, S), BF16), pltpu.SemaphoreType.DMA((N // 2 // T,))],
            flops=15 << 20, limit=8,
        )
        for half in range(2)
    ]
    left = call(left_kernel, shape((C, N, S), BF16), *normed, wl_all, row, tok, flops=1 << 30, limit=8)
    lf = left.reshape(C * N, S)
    lf_got = lax.ppermute(lf, "col", core_swap)

    block = shape((ROWS + EXTRA, Z), F32)
    one = 1400 << 20
    shared = (lf, lf_got, w2)
    spread = [pltpu.VMEM((T // 2, 512, 256), BF16)]
    more = spread + [pltpu.VMEM((ROWS + EXTRA, Z), F32)]
    p0 = call(first_kernel, block, *right[0], *shared, scratch=spread, flops=one)
    p1 = call(next_kernel, block, *right[1], *shared, scratch=spread, flops=one)
    p2 = call(next_kernel, block, *right[2], *shared, scratch=spread, flops=one)
    odd, odd_sent = call(odd_kernel, (block,) * 2, *right[3], p1, *shared, scratch=more, flops=one)
    f1 = lax.ppermute(odd_sent, "col", xh_swap)
    even, even_sent = call(even_kernel, (block,) * 2, *right[4], p0, p2, *shared, scratch=more, flops=one)
    f2 = lax.ppermute(even_sent, "col", xh_swap)
    part = shape((ROWS, Z), BF16)
    out_bias = out_bias.reshape(1, Z)
    y1 = call(final_kernel, part, odd, f1, tok, out_bias)
    y2 = call(final_kernel, part, even, f2, tok, out_bias)

    def home(kept):
        return [(z * 4 + c, (z + kept[c]) % 8 * 4 + z // 2) for z in range(8) for c in range(4)]

    g1 = lax.ppermute(y1, ("row", "col"), home((-1, 1, -3, 3)))
    g2 = lax.ppermute(y2, ("row", "col"), home((-2, 2, 0, 4)))
    return call(assemble_kernel, shape((2 * N, T, Z), BF16), g1, g2, scratch=[pltpu.VMEM((2, ROWS, Z), F32)], limit=4)


def solution(mesh):
    in_specs = (
        P("col", "row", None),
        P("col"),
        P("row"),
        P(),
        P(),
        P(None, "chan"),
        P(),
        P("chan", None),
        P(),
    )
    out_specs = P("col", ("row", "chan"), None)
    return jax.shard_map(program, mesh=mesh, in_specs=in_specs, out_specs=out_specs, check_vma=False)
```

```python
import functools

import jax
import jax.numpy as jnp
from jax import lax
from jax.experimental import pallas as pl
from jax.experimental.pallas import tpu as pltpu
from jax.sharding import PartitionSpec as P


F32 = jnp.float32
BF16 = jnp.bfloat16
VMEM = pl.BlockSpec(memory_space=pltpu.VMEM)
HBM = pl.BlockSpec(memory_space=pltpu.HBM)

S = 512
N = 64
M = 64
C = 32
Z = 128
T = 8
ROWS = N * T
EXTRA = 8


def column_of(row):
    n = row.shape[1]
    r = lax.broadcasted_iota(jnp.int32, (n, n), 0)
    c = lax.broadcasted_iota(jnp.int32, (n, n), 1)
    return jnp.sum(jnp.where(r == c, jnp.broadcast_to(row, (n, n)), 0.0), axis=1, keepdims=True)


def normalize(x, gain, bias):
    values = x.astype(F32)
    center = values - jnp.mean(values, axis=1, keepdims=True)
    spread = jnp.mean(center * center, axis=1, keepdims=True)
    return center * lax.rsqrt(spread + 1e-05) * gain[None] + bias[None]


def tokens_of(tok_ref, start, count):
    token = tok_ref[...].astype(F32)
    t_iota = lax.broadcasted_iota(jnp.int32, (count, N), 0)
    l_iota = lax.broadcasted_iota(jnp.int32, (count, N), 1)
    return jnp.sum(
        jnp.where(l_iota == t_iota + start, jnp.broadcast_to(token, (count, N)), 0.0), axis=1, keepdims=True
    )


def pack_kernel(wl_ref, wo_ref, out_ref):
    out_ref[0:Z, :] = wo_ref[...]
    out_ref[Z : Z + 16, :] = jnp.zeros((16, Z), BF16)
    out_ref[Z : Z + 4, 0:M] = wl_ref[...]


def stack_kernel(a, b, out):
    n = out.shape[0] // 2
    out[:n] = a[...].reshape(out.shape[0] // 2, Z + 16, Z)
    out[n:] = b[...].reshape(out.shape[0] // 2, Z + 16, Z)


def weight_kernel(near, far, wl_out, w2_out):
    packs = [near[i] for i in range(4)] + [far[i] for i in range(4)]
    for i in range(0, 8, 2):
        a, b = (packs[i + j][:Z, :].astype(F32).T.astype(BF16) for j in range(2))
        w2_out[:Z, i * 64 : i * 64 + 128] = jnp.concatenate([a[:, :64], b[:, :64]], axis=1)
        w2_out[Z:, i * 64 : i * 64 + 128] = jnp.concatenate([a[:, 64:], b[:, 64:]], axis=1)
    lefts = jnp.concatenate([pack[Z:, :M] for pack in packs], axis=0)
    r = lax.broadcasted_iota(jnp.int32, (C, 128), 0)
    c = lax.broadcasted_iota(jnp.int32, (C, 128), 1)
    pick = c == r // 4 * 16 + r % 2 * 2 + r // 2 % 2
    wl_out[...] = jnp.dot(pick.astype(F32).astype(BF16), lefts, preferred_element_type=F32).astype(BF16)


def right_kernel(x_ref, row_hbm, tok_hbm, gain_hbm, bias_hbm, wr_hbm, out_ref, buf, row_ref, tok_ref, gain_ref, bias_ref, wr_ref, sems):
    k = lax.axis_index("chan")
    pieces = (
        (x_ref.at[pl.ds(k * T, T)], buf),
        (gain_hbm, gain_ref),
        (bias_hbm, bias_ref),
        (tok_hbm, tok_ref),
        (row_hbm, row_ref),
        (wr_hbm, wr_ref),
    )
    copies = [pltpu.make_async_copy(src, dst, sems.at[i]) for i, (src, dst) in enumerate(pieces)]
    for copy in copies:
        copy.start()
    for copy in copies[1:]:
        copy.wait()
    gain = column_of(gain_ref[...])
    bias = column_of(bias_ref[...])
    token_col = tokens_of(tok_ref, k * T, T)
    weight = token_col * row_ref[...].astype(F32)
    wr = wr_ref[...]
    rows = row_ref[...].astype(F32)
    pad = jnp.concatenate([jnp.broadcast_to(token_col, (T, S)), rows, jnp.zeros((T - 1, S), F32)], axis=0)
    out_ref[T * C :, :] = pad.astype(BF16)
    copies[0].wait()
    for t in range(T):
        normed = normalize(buf[t : t + 1], gain, bias).astype(BF16)
        part = jnp.dot(wr, normed[0], preferred_element_type=F32)
        out_ref[t * C : (t + 1) * C, :] = (part * weight[t : t + 1]).astype(BF16)


def norm_kernel(half, x_ref, gain_ref, bias_ref, out_ref, buf, sems):
    copies = [
        pltpu.make_async_copy(x_ref.at[pl.ds(half * N // 2 + g * T, T)], buf.at[g], sems.at[g])
        for g in range(N // 2 // T)
    ]
    for copy in copies:
        copy.start()
    gain = column_of(gain_ref[...])
    bias = column_of(bias_ref[...])
    for g, copy in enumerate(copies):
        copy.wait()

        def one(t, carry):
            normed = normalize(buf[g, pl.ds(t, 1)], gain, bias)
            out_ref[pl.ds(pl.multiple_of((g * T + t) * M, M), M), :] = normed[0].astype(BF16)
            return carry

        lax.fori_loop(0, T, one, 0, unroll=4)


def left_kernel(n_a, n_b, wl_ref, row_ref, tok_ref, out_ref):
    rep = (
        lax.broadcasted_iota(jnp.int32, (C * T, C), 0) // T == lax.broadcasted_iota(jnp.int32, (C * T, C), 1)
    ).astype(F32).astype(BF16)
    tile = (
        lax.broadcasted_iota(jnp.int32, (M, T * M), 0) == lax.broadcasted_iota(jnp.int32, (M, T * M), 1) % M
    ).astype(F32).astype(BF16)
    tall = jnp.dot(rep, wl_ref[...], preferred_element_type=F32).astype(BF16)
    full = jnp.dot(tall, tile, preferred_element_type=F32)
    own = (
        lax.broadcasted_iota(jnp.int32, (C * T, T * M), 0) % T
        == lax.broadcasted_iota(jnp.int32, (C * T, T * M), 1) // M
    )
    wide = jnp.where(own, full, 0.0).astype(BF16)
    rows = row_ref[...].astype(F32)
    for g in range(N // T):
        weight = tokens_of(tok_ref, g * T, T) * rows
        n_ref, at = (n_a, g) if g < N // T // 2 else (n_b, g - N // T // 2)
        part = jnp.dot(wide, n_ref[at * T * M : (at + 1) * T * M, :], preferred_element_type=F32)
        out_ref[:, g * T : (g + 1) * T, :] = (part.reshape(C, T, S) * weight[None]).astype(BF16)


def pair_block(right, other, lf_own, lf_got, w2_ref, spread, out):
    for n in range(8):
        part = sum(
            lax.dot_general(
                factor[: T * C, :],
                lf[n * 256 : (n + 1) * 256, :],
                (((1,), (1,)), ((), ())),
                preferred_element_type=F32,
            )
            for factor, lf in ((right, lf_own), (other, lf_got))
        ).astype(BF16)
        for t in range(T):
            for u in range(2):
                hi = n * 2 + u
                spread[t // 2, hi * C : (hi + 1) * C, (t % 2) * 128 : (t % 2) * 128 + 128] = part[
                    t * C : (t + 1) * C, u * 128 : (u + 1) * 128
                ]
    low = lax.broadcasted_iota(jnp.int32, (Z, 128), 1) < N
    w2 = w2_ref[...]
    for p in range(T // 2):
        both = jnp.dot(w2, spread[p], preferred_element_type=F32)
        x0, y0 = both[:Z, :128], both[Z:, :128]
        x1, y1 = both[:Z, 128:], both[Z:, 128:]
        pair = jnp.where(low, x0, y1) + pltpu.roll(jnp.where(low, x1, y0), N, 1)
        out[p * 128 : (p + 1) * 128, :] = pair.T
    extra = right[T * C :, :].astype(F32)
    rows = extra[T : T + 1] + other[T * C :, :].astype(F32)[T : T + 1]
    rows_used = jnp.sum(rows, axis=1, keepdims=True)
    high = jnp.floor(rows_used * (1.0 / 64.0))
    rows_used = jnp.where(
        lax.broadcasted_iota(jnp.int32, (EXTRA, Z), 1) < N // 2,
        jnp.broadcast_to(high, (EXTRA, Z)),
        jnp.broadcast_to(rows_used - 64.0 * high, (EXTRA, Z)),
    )
    lane = lax.broadcasted_iota(jnp.int32, (EXTRA, Z), 1)
    out[ROWS:, :] = jnp.where(lane < N, rows_used, jnp.broadcast_to(extra[:EXTRA, :1], (EXTRA, Z)))


def choose(first, a, b, one, two):
    one[...] = jnp.where(first, a, b).astype(one.dtype)
    two[...] = jnp.where(first, b, a).astype(two.dtype)


def core():
    return lax.rem(lax.axis_index("col"), 2)


def at_home():
    return lax.axis_index("col") // 2 == lax.axis_index("row") // 4


def first_kernel(right, other, lf_own, lf_got, w2, out, spread):
    @pl.when(core() == 0)
    def _():
        pair_block(right, other, lf_own, lf_got, w2, spread, out)


def next_kernel(right, other, lf_own, lf_got, w2, out, spread):
    pair_block(right, other, lf_own, lf_got, w2, spread, out)


def odd_kernel(right, other, one, lf_own, lf_got, w2, keep, send, spread, three):
    pair_block(right, other, lf_own, lf_got, w2, spread, three)
    choose(at_home(), three[...], one[...], keep, send)


def even_kernel(right, other, zero, two, lf_own, lf_got, w2, keep, send, spread, last):
    @pl.when(core() == 1)
    def _():
        pair_block(right, other, lf_own, lf_got, w2, spread, last)

    @pl.when(core() == 0)
    def _():
        last[...] = zero[...]

    choose(at_home(), last[...], two[...], keep, send)


def final_kernel(keep, got, tok_ref, bias_ref, out):
    total = keep[...] + got[...].astype(F32)
    tail = total[ROWS:, :]
    rows_used = 64.0 * tail[0:1, 0:1] + tail[0:1, N // 2 : N // 2 + 1]
    second = (tail[:, N : N + 1] > 0.0).astype(F32)
    first = column_of(tok_ref[...].astype(F32))
    count = jnp.maximum(rows_used[None] * first[None] * second[:, :, None], 1.0)
    pairs = total[:ROWS, :].reshape(T, N, Z)
    out[...] = ((pairs + bias_ref[...][None]) / count).reshape(ROWS, Z).astype(BF16)


def assemble_kernel(odd, even, out, flat):
    low = lax.rem(lax.axis_index("row"), 2) == 0
    a, b = odd[...].astype(F32), even[...].astype(F32)
    for h, rows in enumerate((jnp.where(low, b, a), jnp.where(low, a, b))):
        for t in range(T):
            flat[h, pl.ds(t, N, stride=T), :] = rows[t * N : (t + 1) * N]
        out[h * N : (h + 1) * N] = flat[h].reshape(N, T, Z).astype(BF16)


def call(kernel, out, *args, specs=None, scratch=(), flops=0, limit=10):
    leaves = jax.tree.leaves(out)
    bytes_accessed = sum(a.size * a.dtype.itemsize for a in list(args) + leaves)
    return pl.pallas_call(
        kernel,
        out_shape=out,
        in_specs=specs or [VMEM] * len(args),
        out_specs=jax.tree.map(lambda _: VMEM, out),
        scratch_shapes=scratch,
        compiler_params=pltpu.CompilerParams(vmem_limit_bytes=limit << 20),
        cost_estimate=pl.CostEstimate(flops=flops, bytes_accessed=bytes_accessed, transcendentals=0),
    )(*args)


def in_hbm(value):
    return pltpu.with_memory_space_constraint(value, pltpu.HBM)


def shape(dims, dtype):
    return jax.ShapeDtypeStruct(dims, dtype)


def program(x, row_mask, token_mask, gain, bias, wl, wr, wo, out_bias):
    xt = in_hbm(x.transpose(1, 2, 0))
    row = row_mask.reshape(1, S)
    tok = token_mask.reshape(1, N)
    gain, bias = gain.reshape(1, M), bias.reshape(1, M)

    core_swap = [(0, 1), (1, 0), (2, 3), (3, 2)]
    xh_swap = [(0, 2), (1, 3), (2, 0), (3, 1)]

    pack = call(pack_kernel, shape((Z + 16, Z), BF16), wl.T, wo)
    packs = pack
    for step in range(3):
        got = lax.ppermute(packs, "chan", [(c, c ^ (1 << step)) for c in range(8)])
        if step < 2:
            packs = call(stack_kernel, shape((2 << step, Z + 16, Z), BF16), packs, got, limit=4)
    wl_all, w2 = call(weight_kernel, (shape((C, M), BF16), shape((2 * Z, 512), BF16)), packs, got, limit=4)

    small = [in_hbm(a) for a in (row, tok, gain, bias, wr.T)]
    own = call(
        right_kernel, shape((T * C + 16, S), BF16), xt, *small,
        specs=[HBM] * 6,
        scratch=[pltpu.VMEM((T, M, S), BF16)] + [pltpu.VMEM(a.shape, a.dtype) for a in small] + [pltpu.SemaphoreType.DMA((6,))],
        flops=20 << 20, limit=8,
    )

    chains = [own, lax.ppermute(own, "col", core_swap)]
    right = [chains]
    for step in range(4):
        pairs = [(z * 4 + c, (z + 1 - 2 * (c % 2)) % 8 * 4 + c) for z in range(8) for c in range(4) if step < 3 or c % 2]
        chains = [lax.ppermute(chains[i], ("row", "col"), pairs) for i in range(2)]
        right.append(chains)

    normed = [
        call(
            functools.partial(norm_kernel, half), shape((N * M // 2, S), BF16), xt, gain, bias,
            specs=[HBM, VMEM, VMEM],
            scratch=[pltpu.VMEM((N // 2 // T, T, M, S), BF16), pltpu.SemaphoreType.DMA((N // 2 // T,))],
            flops=15 << 20, limit=8,
        )
        for half in range(2)
    ]
    left = call(left_kernel, shape((C, N, S), BF16), *normed, wl_all, row, tok, flops=1 << 30, limit=8)
    lf = left.reshape(C * N, S)
    lf_got = lax.ppermute(lf, "col", core_swap)

    block = shape((ROWS + EXTRA, Z), F32)
    sent = shape((ROWS + EXTRA, Z), BF16)
    one = 1400 << 20
    shared = (lf, lf_got, w2)
    spread = [pltpu.VMEM((T // 2, 512, 256), BF16)]
    more = spread + [pltpu.VMEM((ROWS + EXTRA, Z), F32)]
    p0 = call(first_kernel, block, *right[0], *shared, scratch=spread, flops=one)
    p1 = call(next_kernel, block, *right[1], *shared, scratch=spread, flops=one)
    p2 = call(next_kernel, block, *right[2], *shared, scratch=spread, flops=one)
    odd, odd_sent = call(odd_kernel, (block, sent), *right[3], p1, *shared, scratch=more, flops=one)
    f1 = lax.ppermute(odd_sent, "col", xh_swap)
    even, even_sent = call(even_kernel, (block, sent), *right[4], p0, p2, *shared, scratch=more, flops=one)
    f2 = lax.ppermute(even_sent, "col", xh_swap)
    part = shape((ROWS, Z), BF16)
    out_bias = out_bias.reshape(1, Z)
    y1 = call(final_kernel, part, odd, f1, tok, out_bias)
    y2 = call(final_kernel, part, even, f2, tok, out_bias)

    def home(near, far):
        kept = {(z, c): (far if c // 2 == z // 4 else near)[c % 2] for z in range(8) for c in range(4)}
        return [(z * 4 + c, (z + kept[z, c]) % 8 * 4 + z // 2) for z in range(8) for c in range(4)]

    g1 = lax.ppermute(y1, ("row", "col"), home((-1, 1), (-3, 3)))
    g2 = lax.ppermute(y2, ("row", "col"), home((-2, 2), (0, 4)))
    return call(assemble_kernel, shape((2 * N, T, Z), BF16), g1, g2, scratch=[pltpu.VMEM((2, ROWS, Z), F32)], limit=4)


def solution(mesh):
    in_specs = (
        P("col", "row", None),
        P("col"),
        P("row"),
        P(),
        P(),
        P(None, "chan"),
        P(),
        P("chan", None),
        P(),
    )
    out_specs = P("col", ("row", "chan"), None)
    return jax.shard_map(program, mesh=mesh, in_specs=in_specs, out_specs=out_specs, check_vma=False)
```

```python
import functools

import jax
import jax.numpy as jnp
from jax import lax
from jax.experimental import pallas as pl
from jax.experimental.pallas import tpu as pltpu
from jax.sharding import PartitionSpec as P


F32 = jnp.float32
BF16 = jnp.bfloat16
VMEM = pl.BlockSpec(memory_space=pltpu.VMEM)
HBM = pl.BlockSpec(memory_space=pltpu.HBM)

S = 512
N = 64
M = 64
C = 32
Z = 128
T = 8
ROWS = N * T
EXTRA = 8


def column_of(row):
    n = row.shape[1]
    r = lax.broadcasted_iota(jnp.int32, (n, n), 0)
    c = lax.broadcasted_iota(jnp.int32, (n, n), 1)
    return jnp.sum(jnp.where(r == c, jnp.broadcast_to(row, (n, n)), 0.0), axis=1, keepdims=True)


def normalize(x, gain, bias):
    values = x.astype(F32)
    center = values - jnp.mean(values, axis=1, keepdims=True)
    spread = jnp.mean(center * center, axis=1, keepdims=True)
    return center * lax.rsqrt(spread + 1e-05) * gain[None] + bias[None]


def tokens_of(tok_ref, start, count):
    token = tok_ref[...].astype(F32)
    t_iota = lax.broadcasted_iota(jnp.int32, (count, N), 0)
    l_iota = lax.broadcasted_iota(jnp.int32, (count, N), 1)
    return jnp.sum(
        jnp.where(l_iota == t_iota + start, jnp.broadcast_to(token, (count, N)), 0.0), axis=1, keepdims=True
    )


def pack_kernel(wl_ref, wo_ref, out_ref):
    out_ref[0:Z, :] = wo_ref[...]
    out_ref[Z : Z + 16, :] = jnp.zeros((16, Z), BF16)
    out_ref[Z : Z + 4, 0:M] = wl_ref[...]


def stack_kernel(a, b, out):
    n = out.shape[0] // 2
    out[:n] = a[...].reshape(out.shape[0] // 2, Z + 16, Z)
    out[n:] = b[...].reshape(out.shape[0] // 2, Z + 16, Z)


def weight_kernel(near, far, wl_out, w2_out):
    packs = [near[i] for i in range(4)] + [far[i] for i in range(4)]
    for i in range(0, 8, 2):
        a, b = (packs[i + j][:Z, :].astype(F32).T.astype(BF16) for j in range(2))
        w2_out[:Z, i * 64 : i * 64 + 128] = jnp.concatenate([a[:, :64], b[:, :64]], axis=1)
        w2_out[Z:, i * 64 : i * 64 + 128] = jnp.concatenate([a[:, 64:], b[:, 64:]], axis=1)
    lefts = jnp.concatenate([pack[Z:, :M] for pack in packs], axis=0)
    r = lax.broadcasted_iota(jnp.int32, (C, 128), 0)
    c = lax.broadcasted_iota(jnp.int32, (C, 128), 1)
    pick = c == r // 4 * 16 + r % 2 * 2 + r // 2 % 2
    wl_out[...] = jnp.dot(pick.astype(F32).astype(BF16), lefts, preferred_element_type=F32).astype(BF16)


def right_kernel(x_ref, row_hbm, tok_hbm, gain_hbm, bias_hbm, wr_hbm, out_ref, buf, row_ref, tok_ref, gain_ref, bias_ref, wr_ref, sems):
    k = lax.axis_index("chan")
    pieces = (
        (x_ref.at[pl.ds(k * T, T)], buf),
        (gain_hbm, gain_ref),
        (bias_hbm, bias_ref),
        (tok_hbm, tok_ref),
        (row_hbm, row_ref),
        (wr_hbm, wr_ref),
    )
    copies = [pltpu.make_async_copy(src, dst, sems.at[i]) for i, (src, dst) in enumerate(pieces)]
    for copy in copies:
        copy.start()
    for copy in copies[1:]:
        copy.wait()
    gain = column_of(gain_ref[...])
    bias = column_of(bias_ref[...])
    token_col = tokens_of(tok_ref, k * T, T)
    weight = token_col * row_ref[...].astype(F32)
    wr = wr_ref[...]
    rows = row_ref[...].astype(F32)
    pad = jnp.concatenate([jnp.broadcast_to(token_col, (T, S)), rows, jnp.zeros((T - 1, S), F32)], axis=0)
    out_ref[T * C :, :] = pad.astype(BF16)
    copies[0].wait()
    for t in range(T):
        normed = normalize(buf[t : t + 1], gain, bias).astype(BF16)
        part = jnp.dot(wr, normed[0], preferred_element_type=F32)
        out_ref[t * C : (t + 1) * C, :] = (part * weight[t : t + 1]).astype(BF16)


def norm_kernel(half, x_ref, gain_ref, bias_ref, out_ref, buf, sems):
    copies = [
        pltpu.make_async_copy(x_ref.at[pl.ds(half * N // 2 + g * T, T)], buf.at[g], sems.at[g])
        for g in range(N // 2 // T)
    ]
    for copy in copies:
        copy.start()
    gain = column_of(gain_ref[...])
    bias = column_of(bias_ref[...])
    for g, copy in enumerate(copies):
        copy.wait()

        def one(t, carry):
            normed = normalize(buf[g, pl.ds(t, 1)], gain, bias)
            out_ref[pl.ds(pl.multiple_of((g * T + t) * M, M), M), :] = normed[0].astype(BF16)
            return carry

        lax.fori_loop(0, T, one, 0, unroll=8)


def left_kernel(n_a, n_b, wl_ref, row_ref, tok_ref, out_ref):
    rep = (
        lax.broadcasted_iota(jnp.int32, (C * T, C), 0) // T == lax.broadcasted_iota(jnp.int32, (C * T, C), 1)
    ).astype(F32).astype(BF16)
    tile = (
        lax.broadcasted_iota(jnp.int32, (M, T * M), 0) == lax.broadcasted_iota(jnp.int32, (M, T * M), 1) % M
    ).astype(F32).astype(BF16)
    tall = jnp.dot(rep, wl_ref[...], preferred_element_type=F32).astype(BF16)
    full = jnp.dot(tall, tile, preferred_element_type=F32)
    own = (
        lax.broadcasted_iota(jnp.int32, (C * T, T * M), 0) % T
        == lax.broadcasted_iota(jnp.int32, (C * T, T * M), 1) // M
    )
    wide = jnp.where(own, full, 0.0).astype(BF16)
    rows = row_ref[...].astype(F32)
    for g in range(N // T):
        weight = tokens_of(tok_ref, g * T, T) * rows
        n_ref, at = (n_a, g) if g < N // T // 2 else (n_b, g - N // T // 2)
        part = jnp.dot(wide, n_ref[at * T * M : (at + 1) * T * M, :], preferred_element_type=F32)
        out_ref[:, g * T : (g + 1) * T, :] = (part.reshape(C, T, S) * weight[None]).astype(BF16)


def join_kernel(own, got, out):
    out[0] = own[...]
    out[1] = got[...]


def pair_block(right, other, lf_own, lf_got, w2_ref, spread, out):
    for n in range(8):
        part = sum(
            lax.dot_general(
                factor[: T * C, :],
                lf[n * 256 : (n + 1) * 256, :],
                (((1,), (1,)), ((), ())),
                preferred_element_type=F32,
            )
            for factor, lf in ((right, lf_own), (other, lf_got))
        ).astype(BF16)
        for t in range(T):
            for u in range(2):
                hi = n * 2 + u
                spread[t // 2, hi * C : (hi + 1) * C, (t % 2) * 128 : (t % 2) * 128 + 128] = part[
                    t * C : (t + 1) * C, u * 128 : (u + 1) * 128
                ]
    low = lax.broadcasted_iota(jnp.int32, (Z, 128), 1) < N
    w2 = w2_ref[...]
    for p in range(T // 2):
        both = jnp.dot(w2, spread[p], preferred_element_type=F32)
        x0, y0 = both[:Z, :128], both[Z:, :128]
        x1, y1 = both[:Z, 128:], both[Z:, 128:]
        pair = jnp.where(low, x0, y1) + pltpu.roll(jnp.where(low, x1, y0), N, 1)
        out[p * 128 : (p + 1) * 128, :] = pair.T
    extra = right[T * C :, :].astype(F32)
    rows = extra[T : T + 1] + other[T * C :, :].astype(F32)[T : T + 1]
    rows_used = jnp.sum(rows, axis=1, keepdims=True)
    high = jnp.floor(rows_used * (1.0 / 64.0))
    rows_used = jnp.where(
        lax.broadcasted_iota(jnp.int32, (EXTRA, Z), 1) < N // 2,
        jnp.broadcast_to(high, (EXTRA, Z)),
        jnp.broadcast_to(rows_used - 64.0 * high, (EXTRA, Z)),
    )
    lane = lax.broadcasted_iota(jnp.int32, (EXTRA, Z), 1)
    out[ROWS:, :] = jnp.where(lane < N, rows_used, jnp.broadcast_to(extra[:EXTRA, :1], (EXTRA, Z)))


def choose(first, a, b, one, two):
    one[...] = jnp.where(first, a, b).astype(one.dtype)
    two[...] = jnp.where(first, b, a).astype(two.dtype)


def core():
    return lax.rem(lax.axis_index("col"), 2)


def keeps_three():
    return lax.axis_index("col") // 2 == lax.rem(lax.axis_index("row"), 2)


def keeps_last():
    return lax.axis_index("col") // 2 != lax.axis_index("row") // 4


def first_kernel(right, other, lf_own, lf_got, w2, out, spread):
    @pl.when(core() == 0)
    def _():
        pair_block(right, other, lf_own, lf_got, w2, spread, out)


def next_kernel(right, other, lf_own, lf_got, w2, out, spread):
    pair_block(right, other, lf_own, lf_got, w2, spread, out)


def odd_kernel(right, other, one, lf_own, lf_got, w2, keep, send, spread, three):
    pair_block(right, other, lf_own, lf_got, w2, spread, three)
    choose(keeps_three(), three[...], one[...], keep, send)


def even_kernel(rights, zero, two, lf_own, lf_got, w2, keep, send, spread, last):
    @pl.when(core() == 1)
    def _():
        pair_block(rights.at[0], rights.at[1], lf_own, lf_got, w2, spread, last)

    @pl.when(core() == 0)
    def _():
        last[...] = zero[...]

    choose(keeps_last(), last[...], two[...], keep, send)


def final_kernel(keep, got, tok_ref, bias_ref, out):
    total = keep[...] + got[...].astype(F32)
    tail = total[ROWS:, :]
    rows_used = 64.0 * tail[0:1, 0:1] + tail[0:1, N // 2 : N // 2 + 1]
    second = (tail[:, N : N + 1] > 0.0).astype(F32)
    first = column_of(tok_ref[...].astype(F32))
    count = jnp.maximum(rows_used[None] * first[None] * second[:, :, None], 1.0)
    pairs = total[:ROWS, :].reshape(T, N, Z)
    out[...] = ((pairs + bias_ref[...][None]) / count).reshape(ROWS, Z).astype(BF16)


def place(block, half, out, flat, tile, sem):
    rows = block[...].astype(F32)
    for t in range(T):
        flat[pl.ds(t, N, stride=T), :] = rows[t * N : (t + 1) * N]
    tile[...] = flat[...].reshape(N, T, Z).astype(BF16)
    copy = pltpu.make_async_copy(tile, out.at[pl.ds(half * N, N)], sem)
    copy.start()
    copy.wait()


def odd_half_kernel(block, out, *scratch):
    place(block, 1 - lax.rem(lax.axis_index("row"), 2), out, *scratch)


def even_half_kernel(block, _, out, *scratch):
    place(block, lax.rem(lax.axis_index("row"), 2), out, *scratch)


def call(kernel, out, *args, specs=None, scratch=(), flops=0, limit=10, out_spec=VMEM, alias=None):
    leaves = jax.tree.leaves(out)
    bytes_accessed = sum(a.size * a.dtype.itemsize for a in list(args) + leaves)
    return pl.pallas_call(
        kernel,
        out_shape=out,
        in_specs=specs or [VMEM] * len(args),
        out_specs=jax.tree.map(lambda _: out_spec, out),
        scratch_shapes=scratch,
        input_output_aliases=alias or {},
        compiler_params=pltpu.CompilerParams(vmem_limit_bytes=limit << 20),
        cost_estimate=pl.CostEstimate(flops=flops, bytes_accessed=bytes_accessed, transcendentals=0),
    )(*args)


def in_hbm(value):
    return pltpu.with_memory_space_constraint(value, pltpu.HBM)


def shape(dims, dtype):
    return jax.ShapeDtypeStruct(dims, dtype)


def program(x, row_mask, token_mask, gain, bias, wl, wr, wo, out_bias):
    xt = in_hbm(x.transpose(1, 2, 0))
    row = row_mask.reshape(1, S)
    tok = token_mask.reshape(1, N)
    gain, bias = gain.reshape(1, M), bias.reshape(1, M)

    core_swap = [(0, 1), (1, 0), (2, 3), (3, 2)]
    xh_swap = [(0, 2), (1, 3), (2, 0), (3, 1)]

    pack = call(pack_kernel, shape((Z + 16, Z), BF16), wl.T, wo)
    packs = pack
    for step in range(3):
        got = lax.ppermute(packs, "chan", [(c, c ^ (1 << step)) for c in range(8)])
        if step < 2:
            packs = call(stack_kernel, shape((2 << step, Z + 16, Z), BF16), packs, got, limit=4)
    wl_all, w2 = call(weight_kernel, (shape((C, M), BF16), shape((2 * Z, 512), BF16)), packs, got, limit=4)

    small = [in_hbm(a) for a in (row, tok, gain, bias, wr.T)]
    own = call(
        right_kernel, shape((T * C + 16, S), BF16), xt, *small,
        specs=[HBM] * 6,
        scratch=[pltpu.VMEM((T, M, S), BF16)] + [pltpu.VMEM(a.shape, a.dtype) for a in small] + [pltpu.SemaphoreType.DMA((6,))],
        flops=20 << 20, limit=8,
    )

    chains = [own, lax.ppermute(own, "col", core_swap)]
    right = [chains]
    for step in range(4):
        pairs = [(z * 4 + c, (z + 1 - 2 * (c % 2)) % 8 * 4 + c) for z in range(8) for c in range(4) if step < 3 or c % 2]
        if step == 3:
            both = call(join_kernel, shape((2, T * C + 16, S), BF16), *chains, limit=4)
            chains = [lax.ppermute(both, ("row", "col"), pairs)]
        else:
            chains = [lax.ppermute(chains[i], ("row", "col"), pairs) for i in range(2)]
        right.append(chains)

    normed = [
        call(
            functools.partial(norm_kernel, half), shape((N * M // 2, S), BF16), xt, gain, bias,
            specs=[HBM, VMEM, VMEM],
            scratch=[pltpu.VMEM((N // 2 // T, T, M, S), BF16), pltpu.SemaphoreType.DMA((N // 2 // T,))],
            flops=15 << 20, limit=8,
        )
        for half in range(2)
    ]
    left = call(left_kernel, shape((C, N, S), BF16), *normed, wl_all, row, tok, flops=1 << 30, limit=8)
    lf = left.reshape(C * N, S)
    lf_got = lax.ppermute(lf, "col", core_swap)

    block = shape((ROWS + EXTRA, Z), F32)
    sent = shape((ROWS + EXTRA, Z), BF16)
    one = 1400 << 20
    shared = (lf, lf_got, w2)
    spread = [pltpu.VMEM((T // 2, 512, 256), BF16)]
    more = spread + [pltpu.VMEM((ROWS + EXTRA, Z), F32)]
    p0 = call(first_kernel, block, *right[0], *shared, scratch=spread, flops=one)
    p1 = call(next_kernel, block, *right[1], *shared, scratch=spread, flops=one)
    p2 = call(next_kernel, block, *right[2], *shared, scratch=spread, flops=one)
    odd, odd_sent = call(odd_kernel, (block, sent), *right[3], p1, *shared, scratch=more, flops=one)
    f1 = lax.ppermute(odd_sent, "col", xh_swap)
    even, even_sent = call(even_kernel, (block, sent), *right[4], p0, p2, *shared, scratch=more, flops=one)
    f2 = lax.ppermute(even_sent, "col", xh_swap)
    part = shape((ROWS, Z), BF16)
    out_bias = out_bias.reshape(1, Z)
    y1 = call(final_kernel, part, odd, f1, tok, out_bias)
    y2 = call(final_kernel, part, even, f2, tok, out_bias)

    def home(kept):
        return [(z * 4 + c, (z + kept(z, c // 2)[c % 2]) % 8 * 4 + z // 2) for z in range(8) for c in range(4)]

    g1 = lax.ppermute(y1, ("row", "col"), home(lambda z, x: (-3, 3) if x == z % 2 else (-1, 1)))
    g2 = lax.ppermute(y2, ("row", "col"), home(lambda z, x: (0, 4) if x != z // 4 else (-2, 2)))
    scratch = [pltpu.VMEM((ROWS, Z), F32), pltpu.VMEM((N, T, Z), BF16), pltpu.SemaphoreType.DMA(())]
    whole = shape((2 * N, T, Z), BF16)
    out = call(odd_half_kernel, whole, g1, scratch=scratch, limit=4, out_spec=HBM)
    return call(
        even_half_kernel, whole, g2, out, specs=[VMEM, HBM], scratch=scratch, limit=4, out_spec=HBM, alias={1: 0}
    )


def solution(mesh):
    in_specs = (
        P("col", "row", None),
        P("col"),
        P("row"),
        P(),
        P(),
        P(None, "chan"),
        P(),
        P("chan", None),
        P(),
    )
    out_specs = P("col", ("row", "chan"), None)
    return jax.shard_map(program, mesh=mesh, in_specs=in_specs, out_specs=out_specs, check_vma=False)
```

```python
import functools

import jax
import jax.numpy as jnp
from jax import lax
from jax.experimental import pallas as pl
from jax.experimental.pallas import tpu as pltpu
from jax.sharding import PartitionSpec as P


F32 = jnp.float32
BF16 = jnp.bfloat16
VMEM = pl.BlockSpec(memory_space=pltpu.VMEM)
HBM = pl.BlockSpec(memory_space=pltpu.HBM)

S = 512
N = 64
M = 64
C = 32
Z = 128
T = 8
ROWS = N * T
EXTRA = 8


def column_of(row):
    n = row.shape[1]
    r = lax.broadcasted_iota(jnp.int32, (n, n), 0)
    c = lax.broadcasted_iota(jnp.int32, (n, n), 1)
    return jnp.sum(jnp.where(r == c, jnp.broadcast_to(row, (n, n)), 0.0), axis=1, keepdims=True)


def normalize(x, gain, bias):
    values = x.astype(F32)
    center = values - jnp.mean(values, axis=1, keepdims=True)
    spread = jnp.mean(center * center, axis=1, keepdims=True)
    return center * lax.rsqrt(spread + 1e-05) * gain[None] + bias[None]


def tokens_of(tok_ref, start, count):
    token = tok_ref[...].astype(F32)
    t_iota = lax.broadcasted_iota(jnp.int32, (count, N), 0)
    l_iota = lax.broadcasted_iota(jnp.int32, (count, N), 1)
    return jnp.sum(
        jnp.where(l_iota == t_iota + start, jnp.broadcast_to(token, (count, N)), 0.0), axis=1, keepdims=True
    )


def pack_kernel(wl_ref, wo_ref, out_ref):
    out_ref[0:Z, :] = wo_ref[...]
    out_ref[Z : Z + 16, :] = jnp.zeros((16, Z), BF16)
    out_ref[Z : Z + 4, 0:M] = wl_ref[...]


def stack_kernel(a, b, out):
    n = out.shape[0] // 2
    out[:n] = a[...].reshape(out.shape[0] // 2, Z + 16, Z)
    out[n:] = b[...].reshape(out.shape[0] // 2, Z + 16, Z)


def weight_kernel(near, far, wl_out, w2_out):
    packs = [near[i] for i in range(4)] + [far[i] for i in range(4)]
    for i in range(0, 8, 2):
        a, b = (packs[i + j][:Z, :].astype(F32).T.astype(BF16) for j in range(2))
        w2_out[:Z, i * 64 : i * 64 + 128] = jnp.concatenate([a[:, :64], b[:, :64]], axis=1)
        w2_out[Z:, i * 64 : i * 64 + 128] = jnp.concatenate([a[:, 64:], b[:, 64:]], axis=1)
    lefts = jnp.concatenate([pack[Z:, :M] for pack in packs], axis=0)
    r = lax.broadcasted_iota(jnp.int32, (C, 128), 0)
    c = lax.broadcasted_iota(jnp.int32, (C, 128), 1)
    pick = c == r // 4 * 16 + r % 2 * 2 + r // 2 % 2
    wl_out[...] = jnp.dot(pick.astype(F32).astype(BF16), lefts, preferred_element_type=F32).astype(BF16)


def right_kernel(x_ref, row_hbm, tok_hbm, gain_hbm, bias_hbm, wr_hbm, out_ref, buf, row_ref, tok_ref, gain_ref, bias_ref, wr_ref, sems):
    k = lax.axis_index("chan")
    pieces = (
        (x_ref.at[pl.ds(k * T, T)], buf),
        (gain_hbm, gain_ref),
        (bias_hbm, bias_ref),
        (tok_hbm, tok_ref),
        (row_hbm, row_ref),
        (wr_hbm, wr_ref),
    )
    copies = [pltpu.make_async_copy(src, dst, sems.at[i]) for i, (src, dst) in enumerate(pieces)]
    for copy in copies:
        copy.start()
    for copy in copies[1:]:
        copy.wait()
    gain = column_of(gain_ref[...])
    bias = column_of(bias_ref[...])
    token_col = tokens_of(tok_ref, k * T, T)
    weight = token_col * row_ref[...].astype(F32)
    wr = wr_ref[...]
    rows = row_ref[...].astype(F32)
    pad = jnp.concatenate([jnp.broadcast_to(token_col, (T, S)), rows, jnp.zeros((T - 1, S), F32)], axis=0)
    out_ref[T * C :, :] = pad.astype(BF16)
    copies[0].wait()
    for t in range(T):
        normed = normalize(buf[t : t + 1], gain, bias).astype(BF16)
        part = jnp.dot(wr, normed[0], preferred_element_type=F32)
        out_ref[t * C : (t + 1) * C, :] = (part * weight[t : t + 1]).astype(BF16)


def norm_kernel(half, x_ref, gain_ref, bias_ref, out_ref, buf, sems):
    copies = [
        pltpu.make_async_copy(x_ref.at[pl.ds(half * N // 2 + g * T, T)], buf.at[g], sems.at[g])
        for g in range(N // 2 // T)
    ]
    for copy in copies:
        copy.start()
    gain = column_of(gain_ref[...])
    bias = column_of(bias_ref[...])
    for g, copy in enumerate(copies):
        copy.wait()

        def one(t, carry):
            normed = normalize(buf[g, pl.ds(t, 1)], gain, bias)
            out_ref[pl.ds(pl.multiple_of((g * T + t) * M, M), M), :] = normed[0].astype(BF16)
            return carry

        lax.fori_loop(0, T, one, 0, unroll=8)


def left_kernel(n_a, n_b, wl_ref, row_ref, tok_ref, out_ref):
    rep = (
        lax.broadcasted_iota(jnp.int32, (C * T, C), 0) // T == lax.broadcasted_iota(jnp.int32, (C * T, C), 1)
    ).astype(F32).astype(BF16)
    tile = (
        lax.broadcasted_iota(jnp.int32, (M, T * M), 0) == lax.broadcasted_iota(jnp.int32, (M, T * M), 1) % M
    ).astype(F32).astype(BF16)
    tall = jnp.dot(rep, wl_ref[...], preferred_element_type=F32).astype(BF16)
    full = jnp.dot(tall, tile, preferred_element_type=F32)
    own = (
        lax.broadcasted_iota(jnp.int32, (C * T, T * M), 0) % T
        == lax.broadcasted_iota(jnp.int32, (C * T, T * M), 1) // M
    )
    wide = jnp.where(own, full, 0.0).astype(BF16)
    rows = row_ref[...].astype(F32)
    for g in range(N // T):
        weight = tokens_of(tok_ref, g * T, T) * rows
        n_ref, at = (n_a, g) if g < N // T // 2 else (n_b, g - N // T // 2)
        part = jnp.dot(wide, n_ref[at * T * M : (at + 1) * T * M, :], preferred_element_type=F32)
        out_ref[:, g * T : (g + 1) * T, :] = (part.reshape(C, T, S) * weight[None]).astype(BF16)


def pair_block(right, other, lf_own, lf_got, w2_ref, spread, out):
    for n in range(8):
        part = sum(
            lax.dot_general(
                factor[: T * C, :],
                lf[n * 256 : (n + 1) * 256, :],
                (((1,), (1,)), ((), ())),
                preferred_element_type=F32,
            )
            for factor, lf in ((right, lf_own), (other, lf_got))
        ).astype(BF16)
        for t in range(T):
            for u in range(2):
                hi = n * 2 + u
                spread[t // 2, hi * C : (hi + 1) * C, (t % 2) * 128 : (t % 2) * 128 + 128] = part[
                    t * C : (t + 1) * C, u * 128 : (u + 1) * 128
                ]
    low = lax.broadcasted_iota(jnp.int32, (Z, 128), 1) < N
    w2 = w2_ref[...]
    for p in range(T // 2):
        both = jnp.dot(w2, spread[p], preferred_element_type=F32)
        x0, y0 = both[:Z, :128], both[Z:, :128]
        x1, y1 = both[:Z, 128:], both[Z:, 128:]
        pair = jnp.where(low, x0, y1) + pltpu.roll(jnp.where(low, x1, y0), N, 1)
        out[p * 128 : (p + 1) * 128, :] = pair.T
    extra = right[T * C :, :].astype(F32)
    rows = extra[T : T + 1] + other[T * C :, :].astype(F32)[T : T + 1]
    rows_used = jnp.sum(rows, axis=1, keepdims=True)
    high = jnp.floor(rows_used * (1.0 / 64.0))
    rows_used = jnp.where(
        lax.broadcasted_iota(jnp.int32, (EXTRA, Z), 1) < N // 2,
        jnp.broadcast_to(high, (EXTRA, Z)),
        jnp.broadcast_to(rows_used - 64.0 * high, (EXTRA, Z)),
    )
    lane = lax.broadcasted_iota(jnp.int32, (EXTRA, Z), 1)
    out[ROWS:, :] = jnp.where(lane < N, rows_used, jnp.broadcast_to(extra[:EXTRA, :1], (EXTRA, Z)))


def choose(first, a, b, one, two):
    one[...] = jnp.where(first, a, b).astype(one.dtype)
    two[...] = jnp.where(first, b, a).astype(two.dtype)


def core():
    return lax.rem(lax.axis_index("col"), 2)


def keeps_three():
    return lax.axis_index("col") // 2 == lax.rem(lax.axis_index("row"), 2)


def keeps_last():
    return lax.axis_index("col") // 2 != lax.axis_index("row") // 4


def first_kernel(right, other, lf_own, lf_got, w2, out, spread):
    @pl.when(core() == 0)
    def _():
        pair_block(right, other, lf_own, lf_got, w2, spread, out)


def next_kernel(right, other, lf_own, lf_got, w2, out, spread):
    pair_block(right, other, lf_own, lf_got, w2, spread, out)


def odd_kernel(right, other, one, lf_own, lf_got, w2, keep, send, spread, three):
    pair_block(right, other, lf_own, lf_got, w2, spread, three)
    choose(keeps_three(), three[...], one[...], keep, send)


def even_kernel(right, other, zero, two, lf_own, lf_got, w2, keep, send, spread, last):
    @pl.when(core() == 1)
    def _():
        pair_block(right, other, lf_own, lf_got, w2, spread, last)

    @pl.when(core() == 0)
    def _():
        last[...] = zero[...]

    choose(keeps_last(), last[...], two[...], keep, send)


def final_kernel(keep, got, tok_ref, bias_ref, out):
    total = keep[...] + got[...].astype(F32)
    tail = total[ROWS:, :]
    rows_used = 64.0 * tail[0:1, 0:1] + tail[0:1, N // 2 : N // 2 + 1]
    second = (tail[:, N : N + 1] > 0.0).astype(F32)
    first = column_of(tok_ref[...].astype(F32))
    count = jnp.maximum(rows_used[None] * first[None] * second[:, :, None], 1.0)
    pairs = total[:ROWS, :].reshape(T, N, Z)
    out[...] = ((pairs + bias_ref[...][None]) / count).reshape(ROWS, Z).astype(BF16)


def assemble_kernel(odd, even, out, flat):
    low = lax.rem(lax.axis_index("row"), 2) == 0
    a, b = odd[...].astype(F32), even[...].astype(F32)
    for h, rows in enumerate((jnp.where(low, b, a), jnp.where(low, a, b))):
        for t in range(T):
            flat[h, pl.ds(t, N, stride=T), :] = rows[t * N : (t + 1) * N]
        out[h * N : (h + 1) * N] = flat[h].reshape(N, T, Z).astype(BF16)


def call(kernel, out, *args, specs=None, scratch=(), flops=0, limit=10):
    leaves = jax.tree.leaves(out)
    bytes_accessed = sum(a.size * a.dtype.itemsize for a in list(args) + leaves)
    return pl.pallas_call(
        kernel,
        out_shape=out,
        in_specs=specs or [VMEM] * len(args),
        out_specs=jax.tree.map(lambda _: VMEM, out),
        scratch_shapes=scratch,
        compiler_params=pltpu.CompilerParams(vmem_limit_bytes=limit << 20),
        cost_estimate=pl.CostEstimate(flops=flops, bytes_accessed=bytes_accessed, transcendentals=0),
    )(*args)


def in_hbm(value):
    return pltpu.with_memory_space_constraint(value, pltpu.HBM)


def shape(dims, dtype):
    return jax.ShapeDtypeStruct(dims, dtype)


def program(x, row_mask, token_mask, gain, bias, wl, wr, wo, out_bias):
    xt = in_hbm(x.transpose(1, 2, 0))
    row = row_mask.reshape(1, S)
    tok = token_mask.reshape(1, N)
    gain, bias = gain.reshape(1, M), bias.reshape(1, M)

    core_swap = [(0, 1), (1, 0), (2, 3), (3, 2)]
    xh_swap = [(0, 2), (1, 3), (2, 0), (3, 1)]

    pack = call(pack_kernel, shape((Z + 16, Z), BF16), wl.T, wo)
    packs = pack
    for step in range(3):
        got = lax.ppermute(packs, "chan", [(c, c ^ (1 << step)) for c in range(8)])
        if step < 2:
            packs = call(stack_kernel, shape((2 << step, Z + 16, Z), BF16), packs, got, limit=4)
    wl_all, w2 = call(weight_kernel, (shape((C, M), BF16), shape((2 * Z, 512), BF16)), packs, got, limit=4)

    small = [in_hbm(a) for a in (row, tok, gain, bias, wr.T)]
    own = call(
        right_kernel, shape((T * C + 16, S), BF16), xt, *small,
        specs=[HBM] * 6,
        scratch=[pltpu.VMEM((T, M, S), BF16)] + [pltpu.VMEM(a.shape, a.dtype) for a in small] + [pltpu.SemaphoreType.DMA((6,))],
        flops=20 << 20, limit=8,
    )

    chains = [own, lax.ppermute(own, "col", core_swap)]
    right = [chains]
    for step in range(4):
        pairs = [(z * 4 + c, (z + 1 - 2 * (c % 2)) % 8 * 4 + c) for z in range(8) for c in range(4) if step < 3 or c % 2]
        chains = [lax.ppermute(chains[i], ("row", "col"), pairs) for i in range(2)]
        right.append(chains)

    normed = [
        call(
            functools.partial(norm_kernel, half), shape((N * M // 2, S), BF16), xt, gain, bias,
            specs=[HBM, VMEM, VMEM],
            scratch=[pltpu.VMEM((N // 2 // T, T, M, S), BF16), pltpu.SemaphoreType.DMA((N // 2 // T,))],
            flops=15 << 20, limit=8,
        )
        for half in range(2)
    ]
    left = call(left_kernel, shape((C, N, S), BF16), *normed, wl_all, row, tok, flops=1 << 30, limit=8)
    lf = left.reshape(C * N, S)
    lf_got = lax.ppermute(lf, "col", core_swap)

    block = shape((ROWS + EXTRA, Z), F32)
    sent = shape((ROWS + EXTRA, Z), BF16)
    one = 1400 << 20
    shared = (lf, lf_got, w2)
    spread = [pltpu.VMEM((T // 2, 512, 256), BF16)]
    more = spread + [pltpu.VMEM((ROWS + EXTRA, Z), F32)]
    p0 = call(first_kernel, block, *right[0], *shared, scratch=spread, flops=one)
    p1 = call(next_kernel, block, *right[1], *shared, scratch=spread, flops=one)
    p2 = call(next_kernel, block, *right[2], *shared, scratch=spread, flops=one)
    odd, odd_sent = call(odd_kernel, (block, sent), *right[3], p1, *shared, scratch=more, flops=one)
    f1 = lax.ppermute(odd_sent, "col", xh_swap)
    even, even_sent = call(even_kernel, (block, sent), *right[4], p0, p2, *shared, scratch=more, flops=one)
    f2 = lax.ppermute(even_sent, "col", xh_swap)
    part = shape((ROWS, Z), BF16)
    out_bias = out_bias.reshape(1, Z)
    y1 = call(final_kernel, part, odd, f1, tok, out_bias)
    y2 = call(final_kernel, part, even, f2, tok, out_bias)

    def home(kept):
        return [(z * 4 + c, (z + kept(z, c // 2)[c % 2]) % 8 * 4 + z // 2) for z in range(8) for c in range(4)]

    g1 = lax.ppermute(y1, ("row", "col"), home(lambda z, x: (-3, 3) if x == z % 2 else (-1, 1)))
    g2 = lax.ppermute(y2, ("row", "col"), home(lambda z, x: (0, 4) if x != z // 4 else (-2, 2)))
    return call(assemble_kernel, shape((2 * N, T, Z), BF16), g1, g2, scratch=[pltpu.VMEM((2, ROWS, Z), F32)], limit=4)


def solution(mesh):
    in_specs = (
        P("col", "row", None),
        P("col"),
        P("row"),
        P(),
        P(),
        P(None, "chan"),
        P(),
        P("chan", None),
        P(),
    )
    out_specs = P("col", ("row", "chan"), None)
    return jax.shard_map(program, mesh=mesh, in_specs=in_specs, out_specs=out_specs, check_vma=False)
```
